128 devices in a mesh: lat: 16 (over y_lo, z, core), lon: 4 (over x), rep: 2 (over y_hi).
Axes of the slice: x: 4, y: 4 (y_hi: 2, y_lo: 2; y = y_hi * 2 + y_lo), z: 4, core: 2. Of those that a mesh axis runs over, the one named last changes fastest.
Arguments:
- latent: bfloat16 [6, 96, 384, 512], P('rep', 'lat', 'lon'), parts along dimension 0, may hold values from -6 to 6
- band_labels: int32 [96], replicated, may hold values from 0 to 23, never falling along the last dimension, each value on 1 to 8 neighbouring positions
- gain_first: float32 [512], replicated, may hold values from 0.1 to 1.9
- qkv_first: bfloat16 [512, 1536], replicated, may hold values from -2 to 2
- proj_first: bfloat16 [512, 512], replicated, may hold values from -1 to 1
- merge_gain: float32 [2048], replicated, may hold values from 0.1 to 1.9
- merge_weight: bfloat16 [2048, 1024], replicated, may hold values from -0.125 to 0.125
- gain_coarse: float32 [1024], replicated, may hold values from 0.1 to 1.9
- qkv_coarse: bfloat16 [1024, 3072], replicated, may hold values from -2 to 2
- proj_coarse: bfloat16 [1024, 1024], replicated, may hold values from -0.75 to 0.75
- split_gain: float32 [1024], replicated, may hold values from 0.1 to 1.9
- split_weight: bfloat16 [1024, 2048], replicated, may hold values from -0.1875 to 0.1875
- gain_last: float32 [512], replicated, may hold values from 0.1 to 1.9
- qkv_last: bfloat16 [512, 1536], replicated, may hold values from -2 to 2
- proj_last: bfloat16 [512, 512], replicated, may hold values from -1 to 1
Outputs:
- forecast_latent: bfloat16 [6, 96, 384, 512], P('rep', 'lat', 'lon'), parts along dimension 0
The draws below stay inside these ranges and needn't reach their ends.
There are 2 independent parts, one for each index of `rep`. The reference program is written for one: setup_inputs(seed, part) draws one part's arguments, and reference() takes and returns one part's arrays. A program takes and returns all parts, laid end to end along the dimension named above; an argument that names none is the same for every part. Nothing has to cross between parts.
Inputs may be any that keep to these rules, and one draw needn't show every extreme that they name: `band_labels`: labels never fall along the rows, and each label covers 1 to 8 consecutive rows.
All inputs are finite; a program needn't handle non-finite values.
Results may differ from the reference program's by a relative error of at most 0.015.
Values may be sent and summed in bfloat16 or wider, within the bound.
A program may use at most 128 MiB of HBM per device.

```python
import math
import jax
import jax.numpy as jnp
import numpy as np
from jax import lax

D = 512
HEAD_DIM = 64
LEVELS = 3
WIN_ROWS = 6
WIN_COLS = 12
NLAT = 96
NLON = 384
BANDS = 24


def drawn_projection(key, width):
    base = jax.random.normal(key, (width, 3 * width), jnp.float32) * width ** (-0.5)
    return jnp.clip(base, -2.0, 2.0)


def draw_qkv_first(key, part):
    return drawn_projection(jax.random.fold_in(key, 101), D).astype(jnp.bfloat16)


def draw_qkv_coarse(key, part):
    return drawn_projection(jax.random.fold_in(key, 202), 2 * D).astype(jnp.bfloat16)


def draw_qkv_last(key, part):
    return drawn_projection(jax.random.fold_in(key, 303), D).astype(jnp.bfloat16)


def steps_of(own_key, extent, cuts, low, high):
    level = 1.0
    for position, parts in cuts:
        heights = jax.random.uniform(jax.random.fold_in(jax.random.fold_in(own_key, 6), position), (parts,), jnp.float32, low / len(cuts), high / len(cuts))
        level = level * jnp.repeat(jnp.exp(heights), extent[position] // parts).reshape((-1,) + (1,) * (len(extent) - 1 - position))
    return level


def profile(amount, total, most, lean):
    portions = [(1 << 20) // math.isqrt(rank ** lean) + 1 for rank in range(2, amount + 1)]
    rest, counts = total - most - (amount - 1), [1] * (amount - 1)
    while rest > 0:
        free = [i for i in range(amount - 1) if counts[i] < most]
        pool, remaining = sum([portions[i] for i in free]), rest
        for i in free:
            more = min(most - counts[i], max(1, remaining * portions[i] // pool), rest)
            counts[i] = counts[i] + more
            rest = rest - more
    return np.array([most] + counts)


def uneven(stream_key, amount, total, limit, slope):
    if amount == 2:
        one = jax.random.randint(stream_key, (), max(1, total - limit), min(limit, total - 1) + 1)
        return jnp.stack([one, total - one])
    sizes = jnp.asarray(profile(amount, total, limit, slope), jnp.int32)
    couples = (amount - 1) // 2
    giver, taker = sizes[1:1 + 2 * couples:2], sizes[2:2 + 2 * couples:2]
    room = jnp.minimum(giver - 1, limit - taker)
    shifted = jax.random.randint(jax.random.fold_in(stream_key, 1), (couples,), 0, 1 << 20) % (room + 1)
    sizes = sizes.at[1:1 + 2 * couples:2].set(giver - shifted).at[2:2 + 2 * couples:2].set(taker + shifted)
    return sizes[jax.random.permutation(jax.random.fold_in(stream_key, 2), amount)]


def centred(rng, dims, scale, bound, split=(), dtype=jnp.bfloat16):
    values = jax.random.normal(rng, dims, jnp.float32) * scale
    if len(split) > 0:
        values = steps_of(rng, dims, split, -0.22, 0.18) * values
    return jnp.clip(values, min=-bound, max=bound).astype(dtype)


def setup_inputs(seed: int = 0, part: int = 0) -> dict:
    splits = jax.random.split(jax.random.key(seed), 16)
    own_keys = jax.random.split(jax.random.fold_in(splits[15], part), 16)
    latent = centred(own_keys[0], (LEVELS, NLAT, NLON, D), 1.0, 6.0, ((1, 16), (2, 4)))
    band_labels = jnp.searchsorted(jnp.cumsum(uneven(splits[1], BANDS, NLAT, 8, 0)), jnp.arange(NLAT), side="right").astype(jnp.int32)
    gain_first = jnp.clip(1.0 + 0.18 * jax.random.normal(splits[2], (D,), jnp.float32), 0.1, 1.9)
    qkv_first = draw_qkv_first(jax.random.fold_in(splits[15], 71), part)
    proj_first = centred(splits[4], (D, D), (D // 16) ** -0.5, 1.0)
    merge_gain = jnp.clip(1.0 + 0.18 * jax.random.normal(splits[5], (4 * D,), jnp.float32), 0.1, 1.9)
    merge_weight = centred(splits[6], (4 * D, 2 * D), (4 * D) ** -0.5, 0.125)
    gain_coarse = jnp.clip(1.0 + 0.18 * jax.random.normal(splits[7], (2 * D,), jnp.float32), 0.1, 1.9)
    qkv_coarse = draw_qkv_coarse(jax.random.fold_in(splits[15], 71), part)
    proj_coarse = centred(splits[9], (2 * D, 2 * D), (D // 8) ** -0.5, 0.75)
    split_gain = jnp.clip(1.0 + 0.18 * jax.random.normal(splits[10], (2 * D,), jnp.float32), 0.1, 1.9)
    split_weight = centred(splits[11], (2 * D, 4 * D), (2 * D) ** -0.5, 0.1875)
    gain_last = jnp.clip(1.0 + 0.18 * jax.random.normal(splits[12], (D,), jnp.float32), 0.1, 1.9)
    qkv_last = draw_qkv_last(jax.random.fold_in(splits[15], 71), part)
    proj_last = centred(splits[14], (D, D), (D // 16) ** -0.5, 1.0)
    return {"latent": latent, "band_labels": band_labels, "gain_first": gain_first, "qkv_first": qkv_first, "proj_first": proj_first, "merge_gain": merge_gain, "merge_weight": merge_weight, "gain_coarse": gain_coarse, "qkv_coarse": qkv_coarse, "proj_coarse": proj_coarse, "split_gain": split_gain, "split_weight": split_weight, "gain_last": gain_last, "qkv_last": qkv_last, "proj_last": proj_last}


def layer_norm(values, gain):
    wide = values.astype(jnp.float32)
    center = lax.optimization_barrier(jnp.mean(wide, axis=-1, keepdims=True))
    spread = lax.optimization_barrier(jnp.mean(jnp.square(wide - center), axis=-1, keepdims=True))
    return ((wide - center) * lax.rsqrt(spread + 1e-05) * gain).astype(jnp.bfloat16)

def to_windows(field):
    levels, rows, cols, width = field.shape
    count = cols // WIN_COLS
    shaped = field.reshape(levels, rows, count, WIN_COLS, width).transpose(2, 0, 1, 3, 4)
    return shaped.reshape(count, levels * rows * WIN_COLS, width)

def from_windows(blocks, levels, rows):
    count, tokens, width = blocks.shape
    shaped = blocks.reshape(count, levels, rows, WIN_COLS, width).transpose(1, 2, 0, 3, 4)
    return shaped.reshape(levels, rows, count * WIN_COLS, width)

def token_labels(row_labels):
    rows = row_labels.shape[0]
    return jnp.broadcast_to(row_labels[None, :, None], (LEVELS, rows, WIN_COLS)).reshape(-1)

def attend(queries_in, keys_in, qkv_weight, proj_weight, allowed):
    count, query_tokens, width = queries_in.shape
    key_tokens = keys_in.shape[1]
    heads = width // HEAD_DIM
    query = jnp.dot(queries_in.reshape(-1, width), qkv_weight[:, :width], preferred_element_type=jnp.float32)
    query = query.astype(jnp.bfloat16).reshape(count, query_tokens, heads, HEAD_DIM)
    paired = jnp.dot(keys_in.reshape(-1, width), qkv_weight[:, width:], preferred_element_type=jnp.float32)
    paired = paired.astype(jnp.bfloat16).reshape(count, key_tokens, 2, heads, HEAD_DIM)
    scores = jnp.einsum('wqhd,wkhd->whqk', query.astype(jnp.float32), paired[:, :, 0].astype(jnp.float32))
    scores = scores * HEAD_DIM ** (-0.5)
    scores = jnp.where(allowed[None, None], scores, -1e+30)
    highest = lax.optimization_barrier(jnp.max(scores, axis=-1, keepdims=True))
    expo = jnp.exp(scores - highest)
    weights = (expo / lax.optimization_barrier(jnp.sum(expo, axis=-1, keepdims=True))).astype(jnp.bfloat16)
    mixed = jnp.einsum('whqk,wkhd->wqhd', weights.astype(jnp.float32), paired[:, :, 1].astype(jnp.float32))
    mixed = mixed.astype(jnp.bfloat16).reshape(count * query_tokens, width)
    return jnp.dot(mixed, proj_weight, preferred_element_type=jnp.float32).reshape(count, query_tokens, width)

def shifted_block(field, gain, qkv_weight, proj_weight, labels):
    half_rows = WIN_ROWS // 2
    half_cols = WIN_COLS // 2
    rolled = jnp.roll(field, (-half_rows, -half_cols), axis=(1, 2))
    levels, total_rows, total_cols, width = rolled.shape
    bands = rolled.reshape(levels, total_rows // WIN_ROWS, WIN_ROWS, total_cols, width).transpose(1, 0, 2, 3, 4)
    if labels is None:
        band_rows = jnp.zeros((total_rows // WIN_ROWS, WIN_ROWS), jnp.int32)
    else:
        band_rows = jnp.roll(labels, -half_rows).reshape(-1, WIN_ROWS)

    def one_band(inputs):
        band, row_labels = inputs
        tokens = token_labels(row_labels)
        allowed = tokens[:, None] == tokens[None, :]
        normed = to_windows(layer_norm(band, gain))
        branch = from_windows(attend(normed, normed, qkv_weight, proj_weight, allowed), levels, WIN_ROWS)
        return (band.astype(jnp.float32) + branch).astype(jnp.bfloat16)
    finished = lax.map(one_band, (bands, band_rows))
    finished = finished.transpose(1, 0, 2, 3, 4).reshape(levels, total_rows, total_cols, width)
    return jnp.roll(finished, (half_rows, half_cols), axis=(1, 2))

def merge_tokens(field, gain, weight):
    stacked = jnp.concatenate([field[:, 0::2, 0::2], field[:, 1::2, 0::2], field[:, 0::2, 1::2], field[:, 1::2, 1::2]], axis=-1)
    levels, rows, cols, wide = stacked.shape
    normed = layer_norm(stacked, gain).reshape(-1, wide)
    merged = jnp.dot(normed, weight, preferred_element_type=jnp.float32).astype(jnp.bfloat16)
    return merged.reshape(levels, rows, cols, weight.shape[1])

def split_tokens(coarse, gain, weight, skipped):
    levels, rows, cols, wide = coarse.shape
    normed = layer_norm(coarse, gain).reshape(-1, wide)
    spread = jnp.dot(normed, weight, preferred_element_type=jnp.float32)
    width = weight.shape[1] // 4
    placed = spread.reshape(levels, rows, cols, 2, 2, width).transpose(0, 1, 4, 2, 3, 5)
    placed = placed.reshape(levels, 2 * rows, 2 * cols, width)
    return (skipped.astype(jnp.float32) + placed).astype(jnp.bfloat16)

def reference(latent, band_labels, gain_first, qkv_first, proj_first, merge_gain, merge_weight, gain_coarse, qkv_coarse, proj_coarse, split_gain, split_weight, gain_last, qkv_last, proj_last):
    first = shifted_block(latent, gain_first, qkv_first, proj_first, band_labels)
    merged = merge_tokens(first, merge_gain, merge_weight)
    coarse = shifted_block(merged, gain_coarse, qkv_coarse, proj_coarse, None)
    joined = split_tokens(coarse, split_gain, split_weight, first)
    return shifted_block(joined, gain_last, qkv_last, proj_last, band_labels)
```

```python
import jax
import jax.numpy as jnp
from jax import lax
from jax.experimental import pallas as pl
from jax.experimental.pallas import tpu as pltpu
from jax.sharding import PartitionSpec as P

NT = (((1,), (1,)), ((), ()))
TN = (((0,), (0,)), ((), ()))
f32 = jnp.float32
bf16 = jnp.bfloat16


def norm(x, g):
    c = jnp.mean(x, axis=-1, keepdims=True)
    d = x - c
    s = jnp.mean(d * d, axis=-1, keepdims=True)
    return (d * lax.rsqrt(s + 1e-05) * g).astype(bf16)


def attend_window(x, g, wqkv_ref, wvt_ref, wo_ref, qk_s, vt_s, ot_s, bias_ref):
    E = x.shape[1]
    h = norm(x, g)
    q = jnp.dot(h, wqkv_ref[:, :E], preferred_element_type=f32)
    qk_s[:, :E] = q.astype(bf16) * bf16(0.125)
    k = jnp.dot(h, wqkv_ref[:, E : 2 * E], preferred_element_type=f32)
    qk_s[:, E : 2 * E] = k.astype(bf16)
    vt = lax.dot_general(wvt_ref[...], h, NT, preferred_element_type=f32)
    vt_s[...] = vt.astype(bf16)
    lane = lax.broadcasted_iota(jnp.int32, (216, 128), 1)
    for hp in range(E // 128):
        qb = qk_s[:, 128 * hp : 128 * hp + 128]
        kb = qk_s[:, E + 128 * hp : E + 128 * hp + 128]
        for half in range(2):
            qm = jnp.where((lane >= 64) if half else (lane < 64), qb, bf16(0))
            st = lax.dot_general(kb, qm, NT, preferred_element_type=f32)
            if bias_ref is not None:
                st = st + bias_ref[...]
            m = jnp.max(st, axis=0, keepdims=True)
            e = jnp.exp(st - m)
            d = jnp.sum(e, axis=0, keepdims=True)
            hd = 64 * (2 * hp + half)
            ot = jnp.dot(vt_s[hd : hd + 64, :], e.astype(bf16), preferred_element_type=f32)
            ot_s[hd : hd + 64, :] = (ot * (1.0 / d)).astype(bf16)
    y = lax.dot_general(ot_s[...], wo_ref[...], TN, preferred_element_type=f32)
    return x + y


def token_label(t, lab_ref, start):
    t = t - jnp.where(t >= 144, 144, jnp.where(t >= 72, 72, 0))
    n = lab_ref.shape[0]
    out = jnp.zeros(t.shape, jnp.int32)
    for r in range(6):
        lab = lab_ref[lax.rem(start + r + n, n)]
        out = jnp.where(t >= 12 * r, lab, out)
    return out


def fill_bias(bias_ref, lab_ref, start):
    kt = token_label(lax.broadcasted_iota(jnp.int32, (216, 216), 0), lab_ref, start)
    qt = token_label(lax.broadcasted_iota(jnp.int32, (216, 216), 1), lab_ref, start)
    bias_ref[...] = jnp.where(kt == qt, f32(0), f32(-1e30))


def fine_kernel(lab_ref, x_ref, g_ref, wqkv_ref, wo_ref, o_ref, xw, wvt, bias, qk_s, vt_s, ot_s):
    fill_bias(bias, lab_ref, lax.axis_index("lat") * 6 + 3)
    wvt[...] = wqkv_ref[:, 1024:1536].T
    for lr in range(18):
        slab = x_ref[lr // 6, lr % 6].astype(f32)
        for w in range(8):
            xw[w, 12 * lr : 12 * lr + 12, :] = slab[12 * w : 12 * w + 12]

    def window(w, carry):
        xw[w] = attend_window(xw[w], g_ref[...], wqkv_ref, wvt, wo_ref, qk_s, vt_s, ot_s, bias)
        return carry

    lax.fori_loop(0, 8, window, 0)
    for lr in range(18):
        slab = jnp.concatenate([xw[w, 12 * lr : 12 * lr + 12, :] for w in range(8)], axis=0)
        o_ref[lr // 6, lr % 6] = slab.astype(bf16)


def fine_call(labels, x, g, wqkv, wo):
    V = pl.BlockSpec(memory_space=pltpu.VMEM)
    return pl.pallas_call(
        fine_kernel,
        out_shape=jax.ShapeDtypeStruct(x.shape, bf16),
        in_specs=[pl.BlockSpec(memory_space=pltpu.SMEM), V, V, V, V],
        out_specs=V,
        scratch_shapes=[
            pltpu.VMEM((8, 216, 512), f32),
            pltpu.VMEM((512, 512), bf16),
            pltpu.VMEM((216, 216), f32),
            pltpu.VMEM((216, 1024), bf16),
            pltpu.VMEM((512, 216), bf16),
            pltpu.VMEM((512, 216), bf16),
        ],
        compiler_params=pltpu.CompilerParams(vmem_limit_bytes=60 << 20),
        cost_estimate=pl.CostEstimate(flops=5 * 10**9, bytes_accessed=6 * 10**6, transcendentals=3 * 10**6),
        name="fine",
    )(labels, x, g.reshape(1, -1), wqkv, wo)


def vm():
    return pl.BlockSpec(memory_space=pltpu.VMEM)


def merge_kernel(x_ref, g_ref, w_ref, o_ref, tmp, h_s):
    for i in range(9):
        l, rr = i // 3, i % 3
        for r in range(2):
            for j in range(4):
                tmp[r, j] = x_ref[l, 2 * rr + r, :, 128 * j : 128 * j + 128].astype(f32)
        parts = [tmp[r, j, pl.ds(c, 48, stride=2), :] for c in range(2) for r in range(2) for j in range(4)]
        h_s[48 * i : 48 * i + 48, :] = norm(jnp.concatenate(parts, axis=1), g_ref[...])
    for n in range(4):
        y = jnp.dot(h_s[...], w_ref[:, 256 * n : 256 * n + 256], preferred_element_type=f32).astype(bf16)
        for i in range(9):
            o_ref[i // 3, i % 3, :, 256 * n : 256 * n + 256] = y[48 * i : 48 * i + 48]


def merge_call(x, g, w):
    return pl.pallas_call(
        merge_kernel,
        out_shape=jax.ShapeDtypeStruct((3, 3, 48, 1024), bf16),
        in_specs=[vm()] * 3,
        out_specs=vm(),
        scratch_shapes=[pltpu.VMEM((2, 4, 96, 128), f32), pltpu.VMEM((432, 2048), bf16)],
        compiler_params=pltpu.CompilerParams(vmem_limit_bytes=60 << 20),
        cost_estimate=pl.CostEstimate(flops=2 * 10**9, bytes_accessed=7 * 10**6, transcendentals=10**3),
        name="merge",
    )(x, g.reshape(1, -1), w)


def coarse_kernel(x_ref, g_ref, wqkv_ref, wo_ref, o_ref, xw, wvt, qk_s, vt_s, ot_s):
    wvt[...] = wqkv_ref[:, 2048:3072].T
    for lr in range(18):
        slab = x_ref[lr // 6, lr % 6].astype(f32)
        for w in range(2):
            xw[w, 12 * lr : 12 * lr + 12, :] = slab[12 * w : 12 * w + 12]

    def window(w, carry):
        xw[w] = attend_window(xw[w], g_ref[...], wqkv_ref, wvt, wo_ref, qk_s, vt_s, ot_s, None)
        return carry

    lax.fori_loop(0, 2, window, 0)
    for lr in range(18):
        slab = jnp.concatenate([xw[w, 12 * lr : 12 * lr + 12, :] for w in range(2)], axis=0)
        o_ref[lr // 6, lr % 6] = slab.astype(bf16)


def coarse_call(x, g, wqkv, wo):
    return pl.pallas_call(
        coarse_kernel,
        out_shape=jax.ShapeDtypeStruct(x.shape, bf16),
        in_specs=[vm()] * 4,
        out_specs=vm(),
        scratch_shapes=[
            pltpu.VMEM((2, 216, 1024), f32),
            pltpu.VMEM((1024, 1024), bf16),
            pltpu.VMEM((216, 2048), bf16),
            pltpu.VMEM((1024, 216), bf16),
            pltpu.VMEM((1024, 216), bf16),
        ],
        compiler_params=pltpu.CompilerParams(vmem_limit_bytes=60 << 20),
        cost_estimate=pl.CostEstimate(flops=5 * 10**9, bytes_accessed=11 * 10**6, transcendentals=2 * 10**6),
        name="coarse",
    )(x, g.reshape(1, -1), wqkv, wo)


def split_kernel(c_ref, x_ref, g_ref, w_ref, o_ref, tmp, h_s, sp_s):
    for i in range(9):
        h_s[48 * i : 48 * i + 48, :] = norm(c_ref[i // 3, i % 3].astype(f32), g_ref[...])
    for n in range(8):
        sp_s[:, 256 * n : 256 * n + 256] = jnp.dot(
            h_s[...], w_ref[:, 256 * n : 256 * n + 256], preferred_element_type=f32
        )
    for i in range(9):
        l, rr = i // 3, i % 3
        for p in range(4):
            for j in range(4):
                c = 512 * p + 128 * j
                tmp[p % 2, j, pl.ds(p // 2, 48, stride=2), :] = sp_s[48 * i : 48 * i + 48, c : c + 128]
        for r in range(2):
            for j in range(4):
                c = slice(128 * j, 128 * j + 128)
                o_ref[l, 2 * rr + r, :, c] = (x_ref[l, 2 * rr + r, :, c].astype(f32) + tmp[r, j]).astype(bf16)


def split_call(c, x, g, w):
    return pl.pallas_call(
        split_kernel,
        out_shape=jax.ShapeDtypeStruct(x.shape, bf16),
        in_specs=[vm()] * 4,
        out_specs=vm(),
        scratch_shapes=[
            pltpu.VMEM((2, 4, 96, 128), f32),
            pltpu.VMEM((432, 1024), bf16),
            pltpu.VMEM((432, 2048), f32),
        ],
        compiler_params=pltpu.CompilerParams(vmem_limit_bytes=60 << 20),
        cost_estimate=pl.CostEstimate(flops=2 * 10**9, bytes_accessed=8 * 10**6, transcendentals=10**3),
        name="split",
    )(c, x, g.reshape(1, -1), w)


def shift(value, axis, steps):
    count = lax.axis_size(axis)
    return lax.ppermute(value, axis, [(s, (s + steps) % count) for s in range(count)])


def swap_band(value):
    count = lax.axis_size("lat")
    pairs = [(s, (s + (1 if s % 2 else -1)) % count) for s in range(count)]
    return lax.ppermute(value, "lat", pairs)


def roll_ahead(field):
    wide = jnp.concatenate([field[:, :, 6:], shift(field[:, :, :6], "lon", -1)], axis=2)
    return jnp.concatenate([wide[:, 3:], shift(wide[:, :3], "lat", -1)], axis=1)


def roll_behind(field):
    tall = jnp.concatenate([shift(field[:, -3:], "lat", 1), field[:, :-3]], axis=1)
    return jnp.concatenate([shift(tall[:, :, -6:], "lon", 1), tall[:, :, :-6]], axis=2)


def fine_block(field, gain, qkv, proj, labels):
    return roll_behind(fine_call(labels, roll_ahead(field), gain, qkv, proj))


def coarse_block(merged, gain, qkv, proj):
    odd = lax.axis_index("lat") % 2
    wide = jnp.concatenate([merged[:, :, 6:], shift(merged[:, :, :6], "lon", -1)], axis=2)
    mine = lax.dynamic_slice_in_dim(wide, 24 * (1 - odd), 24, 2)
    other = swap_band(lax.dynamic_slice_in_dim(wide, 24 * odd, 24, 2))
    done = coarse_call(jnp.concatenate([mine, other], axis=1), gain, qkv, proj)
    back = swap_band(done[:, 3:])
    kept = done[:, :3]
    left = jnp.where(odd == 1, kept, back)
    right = jnp.where(odd == 1, back, kept)
    return jnp.concatenate([shift(right[:, :, 18:], "lon", 1), left, right[:, :, :18]], axis=2)


def body(
    latent,
    band_labels,
    gain_first,
    qkv_first,
    proj_first,
    merge_gain,
    merge_weight,
    gain_coarse,
    qkv_coarse,
    proj_coarse,
    split_gain,
    split_weight,
    gain_last,
    qkv_last,
    proj_last,
):
    first = fine_block(latent, gain_first, qkv_first, proj_first, band_labels)
    merged = merge_call(first, merge_gain, merge_weight)
    coarse = coarse_block(merged, gain_coarse, qkv_coarse, proj_coarse)
    joined = split_call(coarse, first, split_gain, split_weight)
    return fine_block(joined, gain_last, qkv_last, proj_last, band_labels)


def solution(mesh):
    return jax.shard_map(
        body,
        mesh=mesh,
        in_specs=(P("rep", "lat", "lon", None),) + (P(),) * 14,
        out_specs=P("rep", "lat", "lon", None),
        check_vma=False,
    )
```

```python
import jax
import jax.numpy as jnp
from jax import lax
from jax.experimental import pallas as pl
from jax.experimental.pallas import tpu as pltpu
from jax.sharding import PartitionSpec as P

NT = (((1,), (1,)), ((), ()))
TN = (((0,), (0,)), ((), ()))
f32 = jnp.float32
bf16 = jnp.bfloat16


def norm(x, g):
    c = jnp.mean(x, axis=-1, keepdims=True)
    d = x - c
    s = jnp.mean(d * d, axis=-1, keepdims=True)
    return (d * lax.rsqrt(s + 1e-05) * g).astype(bf16)


def attend_window(x, g, wqkv_ref, wvt_ref, wo_ref, qk_s, vt_s, ot_s, bias_ref):
    E = x.shape[1]
    h = norm(x, g)
    q = jnp.dot(h, wqkv_ref[:, :E], preferred_element_type=f32)
    qk_s[:, :E] = q.astype(bf16) * bf16(0.125)
    k = jnp.dot(h, wqkv_ref[:, E : 2 * E], preferred_element_type=f32)
    qk_s[:, E : 2 * E] = k.astype(bf16)
    vt = lax.dot_general(wvt_ref[...], h, NT, preferred_element_type=f32)
    vt_s[...] = vt.astype(bf16)
    lane = lax.broadcasted_iota(jnp.int32, (216, 128), 1)
    for hp in range(E // 128):
        qb = qk_s[:, 128 * hp : 128 * hp + 128]
        kb = qk_s[:, E + 128 * hp : E + 128 * hp + 128]
        for half in range(2):
            qm = jnp.where((lane >= 64) if half else (lane < 64), qb, bf16(0))
            st = lax.dot_general(kb, qm, NT, preferred_element_type=f32)
            if bias_ref is not None:
                st = st + bias_ref[...]
            m = jnp.max(st, axis=0, keepdims=True)
            e = jnp.exp(st - m)
            d = jnp.sum(e, axis=0, keepdims=True)
            hd = 64 * (2 * hp + half)
            ot = jnp.dot(vt_s[hd : hd + 64, :], e.astype(bf16), preferred_element_type=f32)
            ot_s[hd : hd + 64, :] = (ot * (1.0 / d)).astype(bf16)
    y = lax.dot_general(ot_s[...], wo_ref[...], TN, preferred_element_type=f32)
    return x + y


def token_label(t, lab_ref, start):
    t = t - jnp.where(t >= 144, 144, jnp.where(t >= 72, 72, 0))
    n = lab_ref.shape[0]
    out = jnp.zeros(t.shape, jnp.int32)
    for r in range(6):
        lab = lab_ref[lax.rem(start + r + n, n)]
        out = jnp.where(t >= 12 * r, lab, out)
    return out


def fill_bias(bias_ref, lab_ref, start):
    kt = token_label(lax.broadcasted_iota(jnp.int32, (216, 216), 0), lab_ref, start)
    qt = token_label(lax.broadcasted_iota(jnp.int32, (216, 216), 1), lab_ref, start)
    bias_ref[...] = jnp.where(kt == qt, f32(0), f32(-1e30))


def vm():
    return pl.BlockSpec(memory_space=pltpu.VMEM)


def mega_kernel(
    lab_ref, x_hbm, g1, w1_hbm, o1_hbm, mg, mw_hbm, gc, wc_hbm, oc_hbm, sg, sw_hbm, g3, w3_hbm, o3_hbm,
    out_ref,
    w1, o1, mw, wc, oc, sw, w3, o3, wvt, wvtc,
    xa, xb, xw, nbuf, ebuf, sedge, jbuf, redge, sedge2, comb, hedge, sedge3,
    hx, tmp, bias, qk_s, vt_s, ot_s, qkc, vtc, otc,
    wsem, own_s, own8_s, s0a, r0a, s0b, r0b, own8_r,
    s1, r1, s1e, r1e, s2, r2, s2e, r2e, s3, r3, s3e, r3e,
):
    i = lax.axis_index("lat")
    c = lax.axis_index("lon")
    n_lat = lax.axis_size("lat")
    n_lon = lax.axis_size("lon")
    o = lax.rem(i, 2)

    def dev(di, dc):
        return {"lat": lax.rem(i + di + n_lat, n_lat), "lon": lax.rem(c + dc + n_lon, n_lon)}

    def remote(src, dst, ssem, rsem, to):
        return pltpu.make_async_remote_copy(
            src_ref=src, dst_ref=dst, send_sem=ssem, recv_sem=rsem, device_id=to,
            device_id_type=pl.DeviceIdType.MESH,
        )

    own = pltpu.make_async_copy(
        x_hbm.at[:, :, pl.ds(pl.multiple_of(48 * (1 - o), 16), 48)], xa.at[:, 3:9], own_s
    )
    own.start()
    weights = [
        pltpu.make_async_copy(a, b, wsem.at[k])
        for k, (a, b) in enumerate(
            ((w1_hbm, w1), (o1_hbm, o1), (mw_hbm, mw), (wc_hbm, wc), (oc_hbm, oc), (sw_hbm, sw), (w3_hbm, w3), (o3_hbm, o3))
        )
    ]
    weights[0].start()
    weights[1].start()

    barrier = pltpu.get_barrier_semaphore()
    side = 1 - 2 * o
    for di, dc in ((-1, 0), (1, 0), (-2, 0), (2, 0), (0, -1), (0, 1), (-1, side), (1, side)):
        pl.semaphore_signal(barrier, inc=1, device_id=dev(di, dc), device_id_type=pl.DeviceIdType.MESH)
    pl.semaphore_wait(barrier, 8)

    def t0a(g):
        return remote(
            x_hbm.at[:, pl.ds(3 * g, 3), pl.ds(pl.multiple_of(48 * o, 16), 48)],
            xa.at[:, pl.ds(9 * (1 - g), 3)], s0a.at[1 - g], r0a.at[1 - g], dev(2 * g - 1, 0),
        )

    def t0b(g):
        return remote(
            x_hbm.at[:, pl.ds(3 * g, 3), pl.ds(pl.multiple_of(48 * (1 - o), 16), 8)],
            xb.at[:, pl.ds(9 * (1 - g), 3)], s0b.at[1 - g], r0b.at[1 - g], dev(2 * g - 1, -o),
        )

    def t0c_remote():
        return remote(x_hbm.at[:, :, 0:8], xb.at[:, 3:9], own8_s, own8_r, dev(0, -1))

    def t0c_local():
        return pltpu.make_async_copy(x_hbm.at[:, :, 48:56], xb.at[:, 3:9], own8_r)

    g_in = 1 - o
    for g in (0, 1):
        t0a(g).start()
        t0b(g).start()

    @pl.when(o == 0)
    def _():
        t0c_remote().start()

    @pl.when(o == 1)
    def _():
        t0c_local().start()

    for copy in weights[2:]:
        copy.start()

    fill_bias(bias.at[0], lab_ref, i * 6 - 3 + n_lat * 6)
    fill_bias(bias.at[1], lab_ref, i * 6 + 3)
    weights[0].wait()
    weights[1].wait()
    wvt[...] = w1[:, 1024:1536].T
    own.wait()

    @pl.when(o == 0)
    def _():
        t0c_remote().wait_recv()

    @pl.when(o == 1)
    def _():
        t0c_local().wait()

    fb = 3 * (1 - o)
    gb = 3 * o

    def chunk_to(k):
        far = jnp.where(o == 1, jnp.where(k == 0, -1, 1), jnp.where(k == 3, 1, -1))
        return lax.rem(k + 1 + 2 * o, 4), far

    def edge1(k):
        m, far = chunk_to(k)
        return remote(sedge.at[:, pl.ds(3 * k, 3)], ebuf.at[:, pl.ds(3 * m, 3)], s1e.at[k], r1e.at[m], dev(far, -o))

    def edge2(k):
        m, far = chunk_to(k)
        return remote(sedge2.at[:, pl.ds(3 * k, 3)], redge.at[:, pl.ds(3 * m, 3)], s2e.at[k], r2e.at[m], dev(far, 1 - o))

    rows1 = remote(
        nbuf.at[:, pl.ds(12 * (1 - o), 3)], nbuf.at[:, pl.ds(12 * o, 3)], s1, r1, dev(2 - 4 * o, 0)
    )
    rows2 = remote(
        jbuf.at[:, pl.ds(12 * o, 3)], jbuf.at[:, pl.ds(12 * (1 - o), 3)], s2, r2, dev(4 * o - 2, 0)
    )

    def group1(s, carry):
        g = (1 - o) * (1 - s) + o * s
        t0a(1 - g).wait_recv()
        t0b(1 - g).wait_recv()
        for lr in range(18):
            a = xa[lr // 6, 6 * g + lr % 6].astype(f32)
            b = xb[lr // 6, 6 * g + lr % 6].astype(f32)
            for w in range(3):
                xw[4 * g + w, 12 * lr : 12 * lr + 12, :] = a[6 + 12 * w : 18 + 12 * w]
            xw[4 * g + 3, 12 * lr : 12 * lr + 6, :] = a[42:48]
            xw[4 * g + 3, 12 * lr + 6 : 12 * lr + 12, :] = b[0:6]

        def window(w, carry):
            z = 4 * g + w
            xw[z] = attend_window(xw[z], g1[...], w1, wvt, o1, qk_s, vt_s, ot_s, bias.at[g])

            @pl.when(w == 0)
            def _():
                for lr in range(18):
                    sedge[lr // 6, 6 * g + lr % 6] = xw[z, 12 * lr : 12 * lr + 8, :].astype(bf16)
                edge1(2 * g).start()
                edge1(2 * g + 1).start()

            return carry

        lax.fori_loop(0, 4, window, 0)
        for lr in range(18):
            slab = jnp.concatenate([xw[4 * g + w, 12 * lr : 12 * lr + 12, :] for w in range(4)], axis=0)
            nbuf[lr // 6, fb + 6 * g + lr % 6] = slab.astype(bf16)

        @pl.when(s == 0)
        def _():
            rows1.start()

        return carry

    lax.fori_loop(0, 2, group1, 0)

    for copy in weights[2:6]:
        copy.wait()
    wvtc[...] = wc[:, 2048:3072].T
    rows1.wait_recv()
    for k in range(4):
        edge1(k).wait_recv()
    for lr in range(18):
        l, rr = lr // 6, lr % 6
        for r in range(2):
            a = nbuf[l, gb + 2 * rr + r].astype(f32)
            b = ebuf[l, 2 * rr + r].astype(f32)
            for j in range(4):
                tmp[r, j, 0:48] = a[:, 128 * j : 128 * j + 128]
                tmp[r, j, 48:56] = b[:, 128 * j : 128 * j + 128]
        for p in range(4):
            for j in range(4):
                v = tmp[p % 2, j, pl.ds(6 + p // 2, 24, stride=2), :]
                col = 512 * p + 128 * j
                for w in range(2):
                    hx[w, 12 * lr : 12 * lr + 12, col : col + 128] = v[12 * w : 12 * w + 12]

    def coarse(w, carry):
        merged = jnp.dot(norm(hx[w], mg[...]), mw[...], preferred_element_type=f32)
        x = merged.astype(bf16).astype(f32)
        y = attend_window(x, gc[...], wc, wvtc, oc, qkc, vtc, otc, None)
        h = norm(y.astype(bf16).astype(f32), sg[...])
        hx[w] = jnp.dot(h, sw[...], preferred_element_type=f32)
        return carry

    lax.fori_loop(0, 2, coarse, 0)
    for lr in range(18):
        l, rr = lr // 6, lr % 6
        for p in range(4):
            for j in range(4):
                col = 512 * p + 128 * j
                v = jnp.concatenate([hx[w, 12 * lr : 12 * lr + 12, col : col + 128] for w in range(2)], axis=0)
                tmp[p % 2, j, pl.ds(6 + p // 2, 24, stride=2), :] = v
        for r in range(2):
            sp = jnp.concatenate([tmp[r, j] for j in range(4)], axis=1)
            a = nbuf[l, gb + 2 * rr + r].astype(f32)
            b = ebuf[l, 2 * rr + r].astype(f32)
            jbuf[l, gb + 2 * rr + r] = (a + sp[0:48]).astype(bf16)
            sedge2[l, 2 * rr + r] = (b + sp[48:56]).astype(bf16)
    for k in range(4):
        edge2(k).start()
    rows2.start()

    weights[6].wait()
    weights[7].wait()
    wvt[...] = w3[:, 1024:1536].T

    def t3(g):
        return remote(
            comb.at[1 - o, :, pl.ds(9 * g, 3)], comb.at[1 - o, :, pl.ds(6 - 3 * g, 3)], s3.at[g], r3.at[1 - g],
            dev(2 * g - 1, 0),
        )

    def edge3(k):
        far = jnp.where(k == 0, -1, jnp.where(k == 3, 1, 0))
        m = lax.rem(k + 1, 2)
        return remote(sedge3.at[:, pl.ds(3 * k, 3)], hedge.at[:, pl.ds(3 * m, 3)], s3e.at[k], r3e.at[m], dev(far, 1))

    def group3(s, carry):
        g = o * (1 - s) + (1 - o) * s

        def landed(k, carry):
            m = 2 * g + k
            remote(sedge2.at[:, pl.ds(0, 3)], redge.at[:, pl.ds(3 * m, 3)], s2e.at[0], r2e.at[m], dev(1, 0)).wait_recv()
            return carry

        lax.fori_loop(0, 2, landed, 0)

        @pl.when(s == 1)
        def _():
            rows2.wait_recv()

        for lr in range(18):
            a = jbuf[lr // 6, fb + 6 * g + lr % 6].astype(f32)
            b = redge[lr // 6, 6 * g + lr % 6].astype(f32)
            xw[4 * g, 12 * lr : 12 * lr + 6, :] = b[0:6]
            xw[4 * g, 12 * lr + 6 : 12 * lr + 12, :] = a[6:12]
            for w in range(1, 4):
                xw[4 * g + w, 12 * lr : 12 * lr + 12, :] = a[12 * w : 12 * w + 12]

        def window(w, carry):
            z = 4 * g + w
            xw[z] = attend_window(xw[z], g3[...], w3, wvt, o3, qk_s, vt_s, ot_s, bias.at[g])
            return carry

        lax.fori_loop(0, 4, window, 0)
        for lr in range(18):
            sedge3[lr // 6, 6 * g + lr % 6] = xw[4 * g + 3, 12 * lr + 4 : 12 * lr + 12, :].astype(bf16)

        @pl.when(o == 0)
        def _():
            edge3(2 * g).start()
            edge3(2 * g + 1).start()

        for lr in range(18):
            slab = jnp.concatenate([xw[4 * g + w, 12 * lr : 12 * lr + 12, :] for w in range(4)], axis=0)
            comb[1 - o, lr // 6, 6 * g + lr % 6] = slab.astype(bf16)
        t3(g).start()
        return carry

    lax.fori_loop(0, 2, group3, 0)

    for g in (0, 1):
        remote(
            comb.at[o, :, pl.ds(0, 3)], comb.at[o, :, pl.ds(3 + 3 * g, 3)], s3.at[g], r3.at[g], dev(1, 0)
        ).wait_recv()
        remote(sedge3.at[:, pl.ds(0, 3)], hedge.at[:, pl.ds(3 * g, 3)], s3e.at[g], r3e.at[g], dev(0, 1)).wait_recv()
    for lr in range(18):
        l, r = lr // 6, lr % 6
        e = hedge[l, r].astype(f32)
        left = comb[0, l, r + 3].astype(f32)
        right = comb[1, l, r + 3].astype(f32)
        out_ref[l, r] = jnp.concatenate([e[2:8], left, right[0:42]], axis=0).astype(bf16)

    for g in (0, 1):
        t0a(1 - g).wait_send()
        t0b(1 - g).wait_send()
        t3(g).wait_send()
    for k in range(4):
        edge1(k).wait_send()
        edge2(k).wait_send()
    rows1.wait_send()
    rows2.wait_send()

    @pl.when(o == 0)
    def _():
        t0c_remote().wait_send()
        for k in range(4):
            edge3(k).wait_send()


def mega_call(x, lab, g1, w1, o1, mg, mw, gc, wc, oc, sg, sw, g3, w3, o3):
    V = vm()
    H = pl.BlockSpec(memory_space=pl.ANY)
    B = lambda *s: pltpu.VMEM(s, bf16)
    F = lambda *s: pltpu.VMEM(s, f32)
    D = pltpu.SemaphoreType.DMA
    weights = [B(*a.shape) for a in (w1, o1, mw, wc, oc, sw, w3, o3)]
    scratch = weights + [
        B(512, 512), B(1024, 1024),
        B(3, 12, 48, 512), B(3, 12, 8, 512), F(8, 216, 512), B(3, 15, 48, 512), B(3, 12, 8, 512), B(3, 12, 8, 512),
        B(3, 15, 48, 512), B(3, 12, 8, 512), B(3, 12, 8, 512), B(2, 3, 12, 48, 512), B(3, 6, 8, 512), B(3, 12, 8, 512),
        F(2, 216, 2048), F(2, 4, 56, 128), F(2, 216, 216), B(216, 1024), B(512, 216), B(512, 216),
        B(216, 2048), B(1024, 216), B(1024, 216),
        D((8,)), D, D, D((2,)), D((2,)), D((2,)), D((2,)), D,
        D, D, D((4,)), D((4,)), D, D, D((4,)), D((4,)), D((2,)), D((2,)), D((4,)), D((2,)),
    ]
    row = lambda g: g.reshape(1, -1)
    return pl.pallas_call(
        mega_kernel,
        out_shape=jax.ShapeDtypeStruct(x.shape, bf16),
        in_specs=[pl.BlockSpec(memory_space=pltpu.SMEM), H, V, H, H, V, H, V, H, H, V, H, V, H, H],
        out_specs=V,
        scratch_shapes=scratch,
        compiler_params=pltpu.CompilerParams(
            vmem_limit_bytes=67043328, collective_id=0, has_side_effects=True
        ),
        name="section",
    )(lab, x, row(g1), w1, o1, row(mg), mw, row(gc), wc, oc, row(sg), sw, row(g3), w3, o3)


def solution(mesh):
    return jax.shard_map(
        mega_call,
        mesh=mesh,
        in_specs=(P("rep", "lat", "lon", None),) + (P(),) * 14,
        out_specs=P("rep", "lat", "lon", None),
        check_vma=False,
    )
```

```python
import jax
import jax.numpy as jnp
from jax import lax
from jax.experimental import pallas as pl
from jax.experimental.pallas import tpu as pltpu
from jax.sharding import PartitionSpec as P

NT = (((1,), (1,)), ((), ()))
TN = (((0,), (0,)), ((), ()))
f32 = jnp.float32
bf16 = jnp.bfloat16


def norm(x, g):
    c = jnp.mean(x, axis=-1, keepdims=True)
    d = x - c
    s = jnp.mean(d * d, axis=-1, keepdims=True)
    return (d * lax.rsqrt(s + 1e-05) * g).astype(bf16)


def attend_windows(n, load, finish, g, wqkv_ref, wvt_ref, wo_ref, qk_s, vt_s, ot_s, bias_ref):
    E = wqkv_ref.shape[0]
    heads = E // 64
    for t in range(n):
        h = norm(load(t), g)
        q = jnp.dot(h, wqkv_ref[:, :E], preferred_element_type=f32)
        qk_s[t, :, :E] = (q * 0.125).astype(bf16)
        k = jnp.dot(h, wqkv_ref[:, E : 2 * E], preferred_element_type=f32)
        qk_s[t, :, E : 2 * E] = k.astype(bf16)
        vt = lax.dot_general(wvt_ref[...], h, NT, preferred_element_type=f32)
        vt_s[t] = vt.astype(bf16)
    lane = lax.broadcasted_iota(jnp.int32, (216, 128), 1)

    def scores(t, h):
        hp = h // 2
        qb = qk_s[t, :, 128 * hp : 128 * hp + 128]
        kb = qk_s[t, :, E + 128 * hp : E + 128 * hp + 128]
        qm = jnp.where((lane >= 64) if h % 2 else (lane < 64), qb, bf16(0))
        st = lax.dot_general(kb, qm, NT, preferred_element_type=f32)
        return st if bias_ref is None else st + bias_ref[...]

    def mix(t, h, e, d):
        ot = jnp.dot(vt_s[t, 64 * h : 64 * h + 64, :], e, preferred_element_type=f32)
        ot_s[t, 64 * h : 64 * h + 64, :] = (ot * d).astype(bf16)
        if h == heads - 1:
            finish(t, lax.dot_general(ot_s[t], wo_ref[...], TN, preferred_element_type=f32))

    items = [(t, h) for t in range(n) for h in range(heads)]
    ready = [scores(*it) for it in items[:2]]
    waiting = []
    for k, it in enumerate(items):
        if k + 2 < len(items):
            ready.append(scores(*items[k + 2]))
        st = ready.pop(0)
        e = jnp.exp(st - jnp.max(st, axis=0, keepdims=True))
        waiting.append((*it, e.astype(bf16), 1.0 / jnp.sum(e, axis=0, keepdims=True)))
        if len(waiting) > 2:
            mix(*waiting.pop(0))
    for args in waiting:
        mix(*args)


def token_label(t, lab_ref, start):
    t = t - jnp.where(t >= 144, 144, jnp.where(t >= 72, 72, 0))
    n = lab_ref.shape[0]
    out = jnp.zeros(t.shape, jnp.int32)
    for r in range(6):
        lab = lab_ref[lax.rem(start + r + n, n)]
        out = jnp.where(t >= 12 * r, lab, out)
    return out


def fill_bias(bias_ref, lab_ref, start):
    kt = token_label(lax.broadcasted_iota(jnp.int32, (216, 216), 0), lab_ref, start)
    qt = token_label(lax.broadcasted_iota(jnp.int32, (216, 216), 1), lab_ref, start)
    bias_ref[...] = jnp.where(kt == qt, f32(0), f32(-1e30))


def vm():
    return pl.BlockSpec(memory_space=pltpu.VMEM)


def mega_kernel(
    lab_ref, x_hbm, g1, w1_hbm, o1_hbm, mg, mw_hbm, gc, wc_hbm, oc_hbm, sg, sw_hbm, g3, w3_hbm, o3_hbm,
    out_ref,
    w1, o1, mw, wc, oc, sw, w3, o3, wvt, wvtc,
    xa, xb, xw, nbuf, ebuf, sedge, jbuf, redge, sedge2, comb, hedge, sedge3,
    hx, xc, tmp, bias, qk_s, vt_s, ot_s, qkc, vtc, otc,
    wsem, own_s, own8_s, s0a, r0a, s0b, r0b, own8_r,
    s1, r1, s1e, r1e, s2, r2, s2e, r2e, s3, r3, s3e, r3e,
):
    i = lax.axis_index("lat")
    c = lax.axis_index("lon")
    n_lat = lax.axis_size("lat")
    n_lon = lax.axis_size("lon")
    o = lax.rem(i, 2)

    def dev(di, dc):
        return {"lat": lax.rem(i + di + n_lat, n_lat), "lon": lax.rem(c + dc + n_lon, n_lon)}

    def remote(src, dst, ssem, rsem, to):
        return pltpu.make_async_remote_copy(
            src_ref=src, dst_ref=dst, send_sem=ssem, recv_sem=rsem, device_id=to,
            device_id_type=pl.DeviceIdType.MESH,
        )

    own = pltpu.make_async_copy(
        x_hbm.at[:, :, pl.ds(pl.multiple_of(48 * (1 - o), 16), 48)], xa.at[:, 3:9], own_s
    )
    own.start()
    weights = [
        pltpu.make_async_copy(a, b, wsem.at[k])
        for k, (a, b) in enumerate(
            ((w1_hbm, w1), (o1_hbm, o1), (mw_hbm, mw), (wc_hbm, wc), (oc_hbm, oc), (sw_hbm, sw), (w3_hbm, w3), (o3_hbm, o3))
        )
    ]
    weights[0].start()
    weights[1].start()

    barrier = pltpu.get_barrier_semaphore()
    side = 1 - 2 * o
    for di, dc in ((-1, 0), (1, 0), (-2, 0), (2, 0), (0, -1), (0, 1), (-1, side), (1, side)):
        pl.semaphore_signal(barrier, inc=1, device_id=dev(di, dc), device_id_type=pl.DeviceIdType.MESH)
    pl.semaphore_wait(barrier, 8)

    def t0a(g):
        return remote(
            x_hbm.at[:, pl.ds(3 * g, 3), pl.ds(pl.multiple_of(48 * o, 16), 48)],
            xa.at[:, pl.ds(9 * (1 - g), 3)], s0a.at[1 - g], r0a.at[1 - g], dev(2 * g - 1, 0),
        )

    def t0b(g):
        return remote(
            x_hbm.at[:, pl.ds(3 * g, 3), pl.ds(pl.multiple_of(48 * (1 - o), 16), 8)],
            xb.at[:, pl.ds(9 * (1 - g), 3)], s0b.at[1 - g], r0b.at[1 - g], dev(2 * g - 1, -o),
        )

    def t0c_remote():
        return remote(x_hbm.at[:, :, 0:8], xb.at[:, 3:9], own8_s, own8_r, dev(0, -1))

    def t0c_local():
        return pltpu.make_async_copy(x_hbm.at[:, :, 48:56], xb.at[:, 3:9], own8_r)

    g_in = 1 - o
    for g in (0, 1):
        t0a(g).start()
        t0b(g).start()

    @pl.when(o == 0)
    def _():
        t0c_remote().start()

    @pl.when(o == 1)
    def _():
        t0c_local().start()

    for copy in weights[2:]:
        copy.start()

    fill_bias(bias.at[0], lab_ref, i * 6 - 3 + n_lat * 6)
    fill_bias(bias.at[1], lab_ref, i * 6 + 3)
    weights[0].wait()
    weights[1].wait()
    wvt[...] = w1[:, 1024:1536].T
    own.wait()

    @pl.when(o == 0)
    def _():
        t0c_remote().wait_recv()

    @pl.when(o == 1)
    def _():
        t0c_local().wait()

    fb = 3 * (1 - o)
    gb = 3 * o

    def chunk_to(k):
        far = jnp.where(o == 1, jnp.where(k == 0, -1, 1), jnp.where(k == 3, 1, -1))
        return lax.rem(k + 1 + 2 * o, 4), far

    def edge1(k):
        m, far = chunk_to(k)
        return remote(sedge.at[:, pl.ds(3 * k, 3)], ebuf.at[:, pl.ds(3 * m, 3)], s1e.at[k], r1e.at[m], dev(far, -o))

    def edge2(k):
        m, far = chunk_to(k)
        return remote(sedge2.at[:, pl.ds(3 * k, 3)], redge.at[:, pl.ds(3 * m, 3)], s2e.at[k], r2e.at[m], dev(far, 1 - o))

    rows1 = remote(
        nbuf.at[:, pl.ds(12 * (1 - o), 3)], nbuf.at[:, pl.ds(12 * o, 3)], s1, r1, dev(2 - 4 * o, 0)
    )
    rows2 = remote(
        jbuf.at[:, pl.ds(12 * o, 3)], jbuf.at[:, pl.ds(12 * (1 - o), 3)], s2, r2, dev(4 * o - 2, 0)
    )

    def group1(s, carry):
        g = (1 - o) * (1 - s) + o * s
        t0a(1 - g).wait_recv()
        t0b(1 - g).wait_recv()
        for lr in range(18):
            a = xa[lr // 6, 6 * g + lr % 6].astype(f32)
            b = xb[lr // 6, 6 * g + lr % 6].astype(f32)
            for w in range(3):
                xw[4 * g + w, 12 * lr : 12 * lr + 12, :] = a[6 + 12 * w : 18 + 12 * w]
            xw[4 * g + 3, 12 * lr : 12 * lr + 6, :] = a[42:48]
            xw[4 * g + 3, 12 * lr + 6 : 12 * lr + 12, :] = b[0:6]

        def finish(t, y):
            xw[4 * g + t] = xw[4 * g + t] + y
            if t == 0:
                for lr in range(18):
                    sedge[lr // 6, 6 * g + lr % 6] = xw[4 * g, 12 * lr : 12 * lr + 8, :].astype(bf16)
                edge1(2 * g).start()
                edge1(2 * g + 1).start()

        attend_windows(4, lambda t: xw[4 * g + t], finish, g1[...], w1, wvt, o1, qk_s, vt_s, ot_s, bias.at[g])
        for lr in range(18):
            slab = jnp.concatenate([xw[4 * g + w, 12 * lr : 12 * lr + 12, :] for w in range(4)], axis=0)
            nbuf[lr // 6, fb + 6 * g + lr % 6] = slab.astype(bf16)

        @pl.when(s == 0)
        def _():
            rows1.start()

        return carry

    lax.fori_loop(0, 2, group1, 0)

    for copy in weights[2:6]:
        copy.wait()
    wvtc[...] = wc[:, 2048:3072].T
    rows1.wait_recv()
    for k in range(4):
        edge1(k).wait_recv()
    for lr in range(18):
        l, rr = lr // 6, lr % 6
        for r in range(2):
            a = nbuf[l, gb + 2 * rr + r].astype(f32)
            b = ebuf[l, 2 * rr + r].astype(f32)
            for j in range(4):
                tmp[r, j, 0:48] = a[:, 128 * j : 128 * j + 128]
                tmp[r, j, 48:56] = b[:, 128 * j : 128 * j + 128]
        for p in range(4):
            for j in range(4):
                v = tmp[p % 2, j, pl.ds(6 + p // 2, 24, stride=2), :]
                col = 512 * p + 128 * j
                for w in range(2):
                    hx[w, 12 * lr : 12 * lr + 12, col : col + 128] = v[12 * w : 12 * w + 12]

    def merged(w):
        m = jnp.dot(norm(hx[w], mg[...]), mw[...], preferred_element_type=f32)
        xc[w] = m.astype(bf16).astype(f32)
        return xc[w]

    def split(w, y):
        h = norm((xc[w] + y).astype(bf16).astype(f32), sg[...])
        hx[w] = jnp.dot(h, sw[...], preferred_element_type=f32)

    attend_windows(2, merged, split, gc[...], wc, wvtc, oc, qkc, vtc, otc, None)
    for lr in range(18):
        l, rr = lr // 6, lr % 6
        for p in range(4):
            for j in range(4):
                col = 512 * p + 128 * j
                v = jnp.concatenate([hx[w, 12 * lr : 12 * lr + 12, col : col + 128] for w in range(2)], axis=0)
                tmp[p % 2, j, pl.ds(6 + p // 2, 24, stride=2), :] = v
        for r in range(2):
            sp = jnp.concatenate([tmp[r, j] for j in range(4)], axis=1)
            a = nbuf[l, gb + 2 * rr + r].astype(f32)
            b = ebuf[l, 2 * rr + r].astype(f32)
            jbuf[l, gb + 2 * rr + r] = (a + sp[0:48]).astype(bf16)
            sedge2[l, 2 * rr + r] = (b + sp[48:56]).astype(bf16)
    for k in range(4):
        edge2(k).start()
    rows2.start()

    weights[6].wait()
    weights[7].wait()
    wvt[...] = w3[:, 1024:1536].T

    def t3(g):
        return remote(
            comb.at[1 - o, :, pl.ds(9 * g, 3)], comb.at[1 - o, :, pl.ds(6 - 3 * g, 3)], s3.at[g], r3.at[1 - g],
            dev(2 * g - 1, 0),
        )

    def edge3(k):
        far = jnp.where(k == 0, -1, jnp.where(k == 3, 1, 0))
        m = lax.rem(k + 1, 2)
        return remote(sedge3.at[:, pl.ds(3 * k, 3)], hedge.at[:, pl.ds(3 * m, 3)], s3e.at[k], r3e.at[m], dev(far, 1))

    def group3(s, carry):
        g = o * (1 - s) + (1 - o) * s

        def landed(k, carry):
            m = 2 * g + k
            remote(sedge2.at[:, pl.ds(0, 3)], redge.at[:, pl.ds(3 * m, 3)], s2e.at[0], r2e.at[m], dev(1, 0)).wait_recv()
            return carry

        lax.fori_loop(0, 2, landed, 0)

        @pl.when(s == 1)
        def _():
            rows2.wait_recv()

        for lr in range(18):
            a = jbuf[lr // 6, fb + 6 * g + lr % 6].astype(f32)
            b = redge[lr // 6, 6 * g + lr % 6].astype(f32)
            xw[4 * g, 12 * lr : 12 * lr + 6, :] = b[0:6]
            xw[4 * g, 12 * lr + 6 : 12 * lr + 12, :] = a[6:12]
            for w in range(1, 4):
                xw[4 * g + w, 12 * lr : 12 * lr + 12, :] = a[12 * w : 12 * w + 12]

        def finish(t, y):
            xw[4 * g + t] = xw[4 * g + t] + y

        attend_windows(4, lambda t: xw[4 * g + t], finish, g3[...], w3, wvt, o3, qk_s, vt_s, ot_s, bias.at[g])
        for lr in range(18):
            sedge3[lr // 6, 6 * g + lr % 6] = xw[4 * g + 3, 12 * lr + 4 : 12 * lr + 12, :].astype(bf16)

        @pl.when(o == 0)
        def _():
            edge3(2 * g).start()
            edge3(2 * g + 1).start()

        for lr in range(18):
            slab = jnp.concatenate([xw[4 * g + w, 12 * lr : 12 * lr + 12, :] for w in range(4)], axis=0)
            comb[1 - o, lr // 6, 6 * g + lr % 6] = slab.astype(bf16)
        t3(g).start()
        return carry

    lax.fori_loop(0, 2, group3, 0)

    for g in (0, 1):
        remote(
            comb.at[o, :, pl.ds(0, 3)], comb.at[o, :, pl.ds(3 + 3 * g, 3)], s3.at[g], r3.at[g], dev(1, 0)
        ).wait_recv()
        remote(sedge3.at[:, pl.ds(0, 3)], hedge.at[:, pl.ds(3 * g, 3)], s3e.at[g], r3e.at[g], dev(0, 1)).wait_recv()
    for lr in range(18):
        l, r = lr // 6, lr % 6
        e = hedge[l, r].astype(f32)
        left = comb[0, l, r + 3].astype(f32)
        right = comb[1, l, r + 3].astype(f32)
        out_ref[l, r] = jnp.concatenate([e[2:8], left, right[0:42]], axis=0).astype(bf16)

    for g in (0, 1):
        t0a(1 - g).wait_send()
        t0b(1 - g).wait_send()
        t3(g).wait_send()
    for k in range(4):
        edge1(k).wait_send()
        edge2(k).wait_send()
    rows1.wait_send()
    rows2.wait_send()

    @pl.when(o == 0)
    def _():
        t0c_remote().wait_send()
        for k in range(4):
            edge3(k).wait_send()


def mega_call(x, lab, g1, w1, o1, mg, mw, gc, wc, oc, sg, sw, g3, w3, o3):
    V = vm()
    H = pl.BlockSpec(memory_space=pl.ANY)
    B = lambda *s: pltpu.VMEM(s, bf16)
    F = lambda *s: pltpu.VMEM(s, f32)
    D = pltpu.SemaphoreType.DMA
    weights = [B(*a.shape) for a in (w1, o1, mw, wc, oc, sw, w3, o3)]
    scratch = weights + [
        B(512, 512), B(1024, 1024),
        B(3, 12, 48, 512), B(3, 12, 8, 512), F(8, 216, 512), B(3, 15, 48, 512), B(3, 12, 8, 512), B(3, 12, 8, 512),
        B(3, 15, 48, 512), B(3, 12, 8, 512), B(3, 12, 8, 512), B(2, 3, 12, 48, 512), B(3, 6, 8, 512), B(3, 12, 8, 512),
        F(2, 216, 2048), F(2, 216, 1024), F(2, 4, 56, 128), F(2, 216, 216), B(4, 216, 1024), B(4, 512, 216), B(4, 512, 216),
        B(2, 216, 2048), B(2, 1024, 216), B(2, 1024, 216),
        D((8,)), D, D, D((2,)), D((2,)), D((2,)), D((2,)), D,
        D, D, D((4,)), D((4,)), D, D, D((4,)), D((4,)), D((2,)), D((2,)), D((4,)), D((2,)),
    ]
    row = lambda g: g.reshape(1, -1)
    return pl.pallas_call(
        mega_kernel,
        out_shape=jax.ShapeDtypeStruct(x.shape, bf16),
        in_specs=[pl.BlockSpec(memory_space=pltpu.SMEM), H, V, H, H, V, H, V, H, H, V, H, V, H, H],
        out_specs=V,
        scratch_shapes=scratch,
        compiler_params=pltpu.CompilerParams(
            vmem_limit_bytes=67043328, collective_id=0, has_side_effects=True
        ),
        name="section",
    )(lab, x, row(g1), w1, o1, row(mg), mw, row(gc), wc, oc, row(sg), sw, row(g3), w3, o3)


def solution(mesh):
    return jax.shard_map(
        mega_call,
        mesh=mesh,
        in_specs=(P("rep", "lat", "lon", None),) + (P(),) * 14,
        out_specs=P("rep", "lat", "lon", None),
        check_vma=False,
    )
```

```python
import functools
import jax
import jax.numpy as jnp
from jax import lax
from jax.experimental import pallas as pl
from jax.experimental.pallas import tpu as pltpu
from jax.sharding import PartitionSpec as P

NT = (((1,), (1,)), ((), ()))
TN = (((0,), (0,)), ((), ()))
f32 = jnp.float32
bf16 = jnp.bfloat16


def norm(x, g):
    c = jnp.mean(x, axis=-1, keepdims=True)
    d = x - c
    s = jnp.mean(d * d, axis=-1, keepdims=True)
    return (d * lax.rsqrt(s + 1e-05) * g).astype(bf16)


LOG2E = 1.4426950408889634


def attend_windows(order, begin, finish, hold, g, wqkv_ref, wvt_ref, wo_ref, q_s, k_s, vt_s, ot_s, bias_ref):
    E = wqkv_ref.shape[0]
    heads = E // 64
    lane = lax.broadcasted_iota(jnp.int32, (256, 128), 1)

    def steps_of(t):
        def normed():
            hold[t] = norm(hold[t], g)

        def query(c):
            y = jnp.dot(hold[t], wqkv_ref[:, c : c + 256], preferred_element_type=f32)
            q_s[t, :216, c : c + 256] = (y * (0.125 * LOG2E)).astype(bf16)

        def key(c):
            y = jnp.dot(hold[t], wqkv_ref[:, E + c : E + c + 256], preferred_element_type=f32)
            k_s[t, :216, c : c + 256] = y.astype(bf16)

        def value(c):
            y = lax.dot_general(wvt_ref[c : c + 256, :], hold[t], NT, preferred_element_type=f32).astype(bf16)
            for h in range(4):
                vt_s[t, c // 64 + h, :64, :216] = y[64 * h : 64 * h + 64]

        steps = list(begin(t)) + [normed]
        for c in range(0, E, 256):
            steps += [functools.partial(f, c) for f in (query, key, value)]
        return steps

    def scores(t, h):
        hp = 128 * (h // 2)
        qm = jnp.where((lane >= 64) if h % 2 else (lane < 64), q_s[t, :, hp : hp + 128], bf16(0))
        st = lax.dot_general(k_s[t, :, hp : hp + 128], qm, NT, preferred_element_type=f32)[:216]
        return st if bias_ref is None else st + bias_ref[...]

    def mix(t, h, e):
        ot = jnp.dot(vt_s[t, h], e, preferred_element_type=f32)
        ot_s[t, 64 * h : 64 * h + 64, :] = (ot[:64] * (1.0 / ot[64:65])).astype(bf16)[:, :216]
        if h == heads - 1:
            return finish(t, lax.dot_general(ot_s[t], wo_ref[...], TN, preferred_element_type=f32)) or []
        return []

    items = [(t, h) for t in order for h in range(heads)]
    for step in steps_of(order[0]):
        step()
    ready = [scores(*it) for it in items[:3]]
    waiting, later = [], []
    for k, (t, h) in enumerate(items):
        if h == 0:
            place = order.index(t) + 1
            todo = steps_of(order[place]) if place < len(order) else []
        if h < heads - 3:
            count = -(-len(todo) // (heads - 3 - h))
            for step in todo[:count]:
                step()
            todo = todo[count:]
        for step in later[:2]:
            step()
        later = later[2:]
        if k + 3 < len(items):
            ready.append(scores(*items[k + 3]))
        st = ready.pop(0)
        e = jnp.exp2(st - jnp.max(st, axis=0, keepdims=True))
        waiting.append((t, h, jnp.concatenate([e, jnp.zeros((40, 256), f32)], axis=0).astype(bf16)))
        if len(waiting) > 3:
            later += mix(*waiting.pop(0))
    for args in waiting:
        later += mix(*args)
    for step in later:
        step()


def token_label(t, lab_ref, start):
    t = t - jnp.where(t >= 144, 144, jnp.where(t >= 72, 72, 0))
    n = lab_ref.shape[0]
    out = jnp.zeros(t.shape, jnp.int32)
    for r in range(6):
        lab = lab_ref[lax.rem(start + r + n, n)]
        out = jnp.where(t >= 12 * r, lab, out)
    return out


def fill_bias(bias_ref, lab_ref, start):
    kt = token_label(lax.broadcasted_iota(jnp.int32, (216, 256), 0), lab_ref, start)
    qt = token_label(lax.broadcasted_iota(jnp.int32, (216, 256), 1), lab_ref, start)
    bias_ref[...] = jnp.where(kt == qt, f32(0), f32(-1e30))


def vm():
    return pl.BlockSpec(memory_space=pltpu.VMEM)


def mega_kernel(
    lab_ref, x_hbm, g1, w1_hbm, o1_hbm, mg, mw_hbm, gc, wc_hbm, oc_hbm, sg, sw_hbm, g3, w3_hbm, o3_hbm,
    out_ref,
    w1, o1, mw, wc, oc, sw, w3, o3, wvt, wvtc,
    xa, xb, xw, nbuf, ebuf, sedge, jbuf, redge, sedge2, comb, hedge, sedge3,
    hx, xc, tmp, etmp, bias, q_s, k_s, vt_s, ot_s, qc, kc, vtc, otc, final,
    wsem, own_s, own8_s, s0a, r0a, s0b, r0b, own8_r,
    s1, r1, s1e, r1e, s2, r2, s2e, r2e, s3, r3, s3e, r3e, osem,
):
    i = lax.axis_index("lat")
    c = lax.axis_index("lon")
    n_lat = lax.axis_size("lat")
    n_lon = lax.axis_size("lon")
    o = lax.rem(i, 2)

    def dev(di, dc):
        return {"lat": lax.rem(i + di + n_lat, n_lat), "lon": lax.rem(c + dc + n_lon, n_lon)}

    def remote(src, dst, ssem, rsem, to):
        return pltpu.make_async_remote_copy(
            src_ref=src, dst_ref=dst, send_sem=ssem, recv_sem=rsem, device_id=to,
            device_id_type=pl.DeviceIdType.MESH,
        )

    own = pltpu.make_async_copy(
        x_hbm.at[:, :, pl.ds(pl.multiple_of(48 * (1 - o), 16), 48)], xa.at[:, 3:9], own_s
    )
    own.start()
    weights = [
        pltpu.make_async_copy(a, b, wsem.at[k])
        for k, (a, b) in enumerate(
            ((w1_hbm, w1), (o1_hbm, o1), (mw_hbm, mw), (wc_hbm, wc), (oc_hbm, oc), (sw_hbm, sw), (w3_hbm, w3), (o3_hbm, o3))
        )
    ]
    weights[0].start()
    weights[1].start()

    barrier = pltpu.get_barrier_semaphore()
    side = 1 - 2 * o
    for di, dc in ((-1, 0), (1, 0), (-2, 0), (2, 0), (0, -1), (0, 1), (-1, side), (1, side)):
        pl.semaphore_signal(barrier, inc=1, device_id=dev(di, dc), device_id_type=pl.DeviceIdType.MESH)
    pl.semaphore_wait(barrier, 8)

    def t0a(g):
        return remote(
            x_hbm.at[:, pl.ds(3 * g, 3), pl.ds(pl.multiple_of(48 * o, 16), 48)],
            xa.at[:, pl.ds(9 * (1 - g), 3)], s0a.at[1 - g], r0a.at[1 - g], dev(2 * g - 1, 0),
        )

    def t0b(g):
        return remote(
            x_hbm.at[:, pl.ds(3 * g, 3), pl.ds(pl.multiple_of(48 * (1 - o), 16), 8)],
            xb.at[:, pl.ds(9 * (1 - g), 3)], s0b.at[1 - g], r0b.at[1 - g], dev(2 * g - 1, -o),
        )

    def t0c_remote():
        return remote(x_hbm.at[:, :, 0:8], xb.at[:, 3:9], own8_s, own8_r, dev(0, -1))

    def t0c_local():
        return pltpu.make_async_copy(x_hbm.at[:, :, 48:56], xb.at[:, 3:9], own8_r)

    g_in = 1 - o
    for g in (0, 1):
        t0a(g).start()
        t0b(g).start()

    @pl.when(o == 0)
    def _():
        t0c_remote().start()

    @pl.when(o == 1)
    def _():
        t0c_local().start()

    for copy in weights[2:]:
        copy.start()

    for v in (vt_s, vtc):
        n, heads = v.shape[:2]
        v[:, :, 64:80, :] = jnp.ones((n, heads, 16, 256), bf16)
        v[:, :, :64, 128:256] = jnp.zeros((n, heads, 64, 128), bf16)
    fill_bias(bias.at[0], lab_ref, i * 6 - 3 + n_lat * 6)
    fill_bias(bias.at[1], lab_ref, i * 6 + 3)
    weights[0].wait()
    weights[1].wait()
    wvt[...] = w1[:, 1024:1536].T
    own.wait()

    @pl.when(o == 0)
    def _():
        t0c_remote().wait_recv()

    @pl.when(o == 1)
    def _():
        t0c_local().wait()

    fb = 3 * (1 - o)
    gb = 3 * o

    def chunk_to(k):
        far = jnp.where(o == 1, jnp.where(k == 0, -1, 1), jnp.where(k == 3, 1, -1))
        return lax.rem(k + 1 + 2 * o, 4), far

    def edge1(k):
        m, far = chunk_to(k)
        return remote(sedge.at[:, pl.ds(3 * k, 3)], ebuf.at[:, pl.ds(3 * m, 3)], s1e.at[k], r1e.at[m], dev(far, -o))

    def edge2(k):
        m, far = chunk_to(k)
        return remote(sedge2.at[:, pl.ds(3 * k, 3)], redge.at[:, pl.ds(3 * m, 3)], s2e.at[k], r2e.at[m], dev(far, 1 - o))

    rows1 = remote(
        nbuf.at[:, pl.ds(12 * (1 - o), 3)], nbuf.at[:, pl.ds(12 * o, 3)], s1, r1, dev(2 - 4 * o, 0)
    )
    rows2 = remote(
        jbuf.at[:, pl.ds(12 * o, 3)], jbuf.at[:, pl.ds(12 * (1 - o), 3)], s2, r2, dev(4 * o - 2, 0)
    )

    def group1(s, carry):
        g = (1 - o) * (1 - s) + o * s
        t0a(1 - g).wait_recv()
        t0b(1 - g).wait_recv()
        for lr in range(18):
            a = xa[lr // 6, 6 * g + lr % 6].astype(f32)
            b = xb[lr // 6, 6 * g + lr % 6].astype(f32)
            for w in range(3):
                xw[4 * g + w, 12 * lr : 12 * lr + 12, :] = a[6 + 12 * w : 18 + 12 * w]
            xw[4 * g + 3, 12 * lr : 12 * lr + 6, :] = a[42:48]
            xw[4 * g + 3, 12 * lr + 6 : 12 * lr + 12, :] = b[0:6]

        def finish(t, y):
            xw[4 * g + t] = xw[4 * g + t] + y
            if t == 0:
                for lr in range(18):
                    sedge[lr // 6, 6 * g + lr % 6] = xw[4 * g, 12 * lr : 12 * lr + 8, :].astype(bf16)
                edge1(2 * g).start()
                edge1(2 * g + 1).start()

        hold = {}

        def begin(t):
            def take():
                hold[t] = xw[4 * g + t]

            return [take]

        attend_windows([0, 1, 2, 3], begin, finish, hold, g1[...], w1, wvt, o1, q_s, k_s, vt_s, ot_s, bias.at[g])
        for lr in range(18):
            slab = jnp.concatenate([xw[4 * g + w, 12 * lr : 12 * lr + 12, :] for w in range(4)], axis=0)
            nbuf[lr // 6, fb + 6 * g + lr % 6] = slab.astype(bf16)

        @pl.when(s == 0)
        def _():
            rows1.start()

        return carry

    lax.fori_loop(0, 2, group1, 0)

    for copy in weights[2:6]:
        copy.wait()
    wvtc[...] = wc[:, 2048:3072].T
    rows1.wait_recv()
    for k in range(4):
        edge1(k).wait_recv()
    for lr in range(18):
        l, rr = lr // 6, lr % 6
        for r in range(2):
            a = nbuf[l, gb + 2 * rr + r].astype(f32)
            b = ebuf[l, 2 * rr + r].astype(f32)
            for j in range(4):
                tmp[lr % 2, r, j, 0:48] = a[:, 128 * j : 128 * j + 128]
                tmp[lr % 2, r, j, 48:56] = b[:, 128 * j : 128 * j + 128]
        for p in range(4):
            for j in range(4):
                v = tmp[lr % 2, p % 2, j, pl.ds(6 + p // 2, 24, stride=2), :]
                col = 512 * p + 128 * j
                for w in range(2):
                    hx[w, 12 * lr : 12 * lr + 12, col : col + 128] = v[12 * w : 12 * w + 12]

    hold = {}

    def merge(w):
        def stacked():
            hold[w] = norm(hx[w], mg[...])

        def product(c):
            m = jnp.dot(hold[w], mw[:, c : c + 256], preferred_element_type=f32)
            xc[w, :, c : c + 256] = m.astype(bf16).astype(f32)

        def take():
            hold[w] = xc[w]

        return [stacked] + [functools.partial(product, c) for c in range(0, 1024, 256)] + [take]

    def split(w, y):
        def stacked():
            hold[w] = norm((xc[w] + y).astype(bf16).astype(f32), sg[...])

        def product(c):
            hx[w, :, c : c + 256] = jnp.dot(hold[w], sw[:, c : c + 256], preferred_element_type=f32)

        def edges():
            for lr in range(18):
                l, rr = lr // 6, lr % 6
                for p in range(4):
                    for j in range(4):
                        col = 512 * p + 128 * j
                        etmp[lr, p % 2, j, pl.ds(p // 2, 3, stride=2), :] = hx[1, 12 * lr + 9 : 12 * lr + 12, col : col + 128]
                for r in range(2):
                    sp = jnp.concatenate([etmp[lr, r, j] for j in range(4)], axis=1)
                    sedge2[l, 2 * rr + r] = (ebuf[l, 2 * rr + r].astype(f32) + sp).astype(bf16)
            for k in range(4):
                edge2(k).start()

        steps = [stacked] + [functools.partial(product, c) for c in range(0, 2048, 256)]
        return steps + [edges] if w == 1 else steps

    attend_windows([1, 0], merge, split, hold, gc[...], wc, wvtc, oc, qc, kc, vtc, otc, None)
    for lr in range(18):
        l, rr = lr // 6, lr % 6
        for p in range(4):
            for j in range(4):
                col = 512 * p + 128 * j
                v = jnp.concatenate([hx[w, 12 * lr : 12 * lr + 12, col : col + 128] for w in range(2)], axis=0)
                tmp[lr % 2, p % 2, j, pl.ds(6 + p // 2, 24, stride=2), :] = v
        for r in range(2):
            sp = jnp.concatenate([tmp[lr % 2, r, j] for j in range(4)], axis=1)
            a = nbuf[l, gb + 2 * rr + r].astype(f32)
            jbuf[l, gb + 2 * rr + r] = (a + sp[0:48]).astype(bf16)
    rows2.start()

    weights[6].wait()
    weights[7].wait()
    wvt[...] = w3[:, 1024:1536].T

    def t3(g, half):
        return remote(
            comb.at[1 - o, half, :, pl.ds(9 * g, 3)], comb.at[1 - o, half, :, pl.ds(6 - 3 * g, 3)],
            s3.at[2 * g + half], r3.at[2 * (1 - g) + half], dev(2 * g - 1, 0),
        )

    def edge3(k):
        far = jnp.where(k == 0, -1, jnp.where(k == 3, 1, 0))
        m = lax.rem(k + 1, 2)
        return remote(sedge3.at[:, pl.ds(3 * k, 3)], hedge.at[:, pl.ds(3 * m, 3)], s3e.at[k], r3e.at[m], dev(far, 1))

    def group3(s, carry):
        g = o * (1 - s) + (1 - o) * s

        def landed(k, carry):
            m = 2 * g + k
            remote(sedge2.at[:, pl.ds(0, 3)], redge.at[:, pl.ds(3 * m, 3)], s2e.at[0], r2e.at[m], dev(1, 0)).wait_recv()
            return carry

        lax.fori_loop(0, 2, landed, 0)

        @pl.when(s == 1)
        def _():
            rows2.wait_recv()

        for lr in range(18):
            a = jbuf[lr // 6, fb + 6 * g + lr % 6].astype(f32)
            b = redge[lr // 6, 6 * g + lr % 6].astype(f32)
            xw[4 * g, 12 * lr : 12 * lr + 6, :] = b[0:6]
            xw[4 * g, 12 * lr + 6 : 12 * lr + 12, :] = a[6:12]
            for w in range(1, 4):
                xw[4 * g + w, 12 * lr : 12 * lr + 12, :] = a[12 * w : 12 * w + 12]

        def finish(t, y):
            xw[4 * g + t] = xw[4 * g + t] + y
            if t == 3:
                for lr in range(18):
                    sedge3[lr // 6, 6 * g + lr % 6] = xw[4 * g + 3, 12 * lr + 4 : 12 * lr + 12, :].astype(bf16)

                @pl.when(o == 0)
                def _():
                    edge3(2 * g).start()
                    edge3(2 * g + 1).start()

            if t % 2 == 1:
                for lr in range(18):
                    pair = [xw[4 * g + w, 12 * lr : 12 * lr + 12, :] for w in (t - 1, t)]
                    comb[1 - o, t // 2, lr // 6, 6 * g + lr % 6] = jnp.concatenate(pair, axis=0).astype(bf16)
                t3(g, t // 2).start()

        hold = {}

        def begin(t):
            def take():
                hold[t] = xw[4 * g + t]

            return [take]

        attend_windows([0, 1, 2, 3], begin, finish, hold, g3[...], w3, wvt, o3, q_s, k_s, vt_s, ot_s, bias.at[g])
        return carry

    lax.fori_loop(0, 2, group3, 0)

    def out_copy(b):
        return pltpu.make_async_copy(final.at[:, pl.ds(3 * b, 3)], out_ref.at[:, pl.ds(3 * b, 3)], osem.at[b])

    def assemble(s, carry):
        b = o * (1 - s) + (1 - o) * s
        for half in range(2):
            remote(
                comb.at[o, half, :, pl.ds(0, 3)], comb.at[o, half, :, pl.ds(3 + 3 * b, 3)], s3.at[0], r3.at[2 * b + half],
                dev(1, 0),
            ).wait_recv()
        remote(sedge3.at[:, pl.ds(0, 3)], hedge.at[:, pl.ds(3 * b, 3)], s3e.at[0], r3e.at[b], dev(0, 1)).wait_recv()
        for lr in range(9):
            l, r = lr // 3, 3 * b + lr % 3
            halves = [comb[k, half, l, r + 3].astype(f32) for k in range(2) for half in range(2)]
            parts = [hedge[l, r].astype(f32)[2:8]] + halves[:3] + [halves[3][0:18]]
            final[l, r] = jnp.concatenate(parts, axis=0).astype(bf16)
        out_copy(b).start()
        return carry

    lax.fori_loop(0, 2, assemble, 0)

    for g in (0, 1):
        t0a(1 - g).wait_send()
        t0b(1 - g).wait_send()
        t3(g, 0).wait_send()
        t3(g, 1).wait_send()
        out_copy(g).wait()
    for k in range(4):
        edge1(k).wait_send()
        edge2(k).wait_send()
    rows1.wait_send()
    rows2.wait_send()

    @pl.when(o == 0)
    def _():
        t0c_remote().wait_send()
        for k in range(4):
            edge3(k).wait_send()


def mega_call(x, lab, g1, w1, o1, mg, mw, gc, wc, oc, sg, sw, g3, w3, o3):
    V = vm()
    H = pl.BlockSpec(memory_space=pl.ANY)
    B = lambda *s: pltpu.VMEM(s, bf16)
    F = lambda *s: pltpu.VMEM(s, f32)
    D = pltpu.SemaphoreType.DMA
    weights = [B(*a.shape) for a in (w1, o1, mw, wc, oc, sw, w3, o3)]
    scratch = weights + [
        B(512, 512), B(1024, 1024),
        B(3, 12, 48, 512), B(3, 12, 8, 512), F(8, 216, 512), B(3, 15, 48, 512), B(3, 12, 8, 512), B(3, 12, 8, 512),
        B(3, 15, 48, 512), B(3, 12, 8, 512), B(3, 12, 8, 512), B(2, 2, 3, 12, 24, 512), B(3, 6, 8, 512), B(3, 12, 8, 512),
        F(2, 216, 2048), F(2, 216, 1024), F(2, 2, 4, 56, 128), F(18, 2, 4, 8, 128), F(2, 216, 256),
        B(4, 256, 512), B(4, 224, 512), B(4, 8, 80, 256), B(4, 512, 216),
        B(2, 256, 1024), B(2, 224, 1024), B(2, 16, 80, 256), B(2, 1024, 216), B(3, 6, 96, 512),
        D((8,)), D, D, D((2,)), D((2,)), D((2,)), D((2,)), D,
        D, D, D((4,)), D((4,)), D, D, D((4,)), D((4,)), D((4,)), D((4,)), D((4,)), D((2,)), D((2,)),
    ]
    row = lambda g: g.reshape(1, -1)
    return pl.pallas_call(
        mega_kernel,
        out_shape=jax.ShapeDtypeStruct(x.shape, bf16),
        in_specs=[pl.BlockSpec(memory_space=pltpu.SMEM), H, V, H, H, V, H, V, H, H, V, H, V, H, H],
        out_specs=H,
        scratch_shapes=scratch,
        compiler_params=pltpu.CompilerParams(
            vmem_limit_bytes=67043328, collective_id=0, has_side_effects=True
        ),
        name="section",
    )(lab, x, row(g1), w1, o1, row(mg), mw, row(gc), wc, oc, row(sg), sw, row(g3), w3, o3)


def solution(mesh):
    return jax.shard_map(
        mega_call,
        mesh=mesh,
        in_specs=(P("rep", "lat", "lon", None),) + (P(),) * 14,
        out_specs=P("rep", "lat", "lon", None),
        check_vma=False,
    )
```

```python
import functools
import jax
import jax.numpy as jnp
from jax import lax
from jax.experimental import pallas as pl
from jax.experimental.pallas import tpu as pltpu
from jax.sharding import PartitionSpec as P

NT = (((1,), (1,)), ((), ()))
TN = (((0,), (0,)), ((), ()))
f32 = jnp.float32
bf16 = jnp.bfloat16


def norm(x, g):
    c = jnp.mean(x, axis=-1, keepdims=True)
    d = x - c
    s = jnp.mean(d * d, axis=-1, keepdims=True)
    return (d * lax.rsqrt(s + 1e-05) * g).astype(bf16)


LOG2E = 1.4426950408889634


def attend_windows(order, begin, finish, hold, g, wqkv_ref, wvt_ref, wo_ref, q_s, k_s, vt_s, ot_s, bias_ref):
    E = wqkv_ref.shape[0]
    heads = E // 64
    lane = lax.broadcasted_iota(jnp.int32, (256, 128), 1)

    def steps_of(t):
        def normed():
            hold[t] = norm(hold[t], g)

        def query(c):
            y = jnp.dot(hold[t], wqkv_ref[:, c : c + 256], preferred_element_type=f32)
            q_s[t, :216, c : c + 256] = (y * (0.125 * LOG2E)).astype(bf16)

        def key(c):
            y = jnp.dot(hold[t], wqkv_ref[:, E + c : E + c + 256], preferred_element_type=f32)
            k_s[t, :216, c : c + 256] = y.astype(bf16)

        def value(c):
            y = lax.dot_general(wvt_ref[c : c + 256, :], hold[t], NT, preferred_element_type=f32).astype(bf16)
            for h in range(4):
                vt_s[t, c // 64 + h, :64, :216] = y[64 * h : 64 * h + 64]

        steps = list(begin(t)) + [normed]
        for c in range(0, E, 256):
            steps += [functools.partial(f, c) for f in (query, key, value)]
        return steps

    def scores(t, h):
        hp = 128 * (h // 2)
        qm = jnp.where((lane >= 64) if h % 2 else (lane < 64), q_s[t, :, hp : hp + 128], bf16(0))
        st = lax.dot_general(k_s[t, :, hp : hp + 128], qm, NT, preferred_element_type=f32)[:216]
        return st if bias_ref is None else st + bias_ref[...]

    def mix(t, h, e):
        ot = jnp.dot(vt_s[t, h], e, preferred_element_type=f32)
        ot_s[t, 64 * h : 64 * h + 64, :] = (ot[:64] * (1.0 / ot[64:65])).astype(bf16)[:, :216]
        if h == heads - 1:
            return finish(t, lax.dot_general(ot_s[t], wo_ref[...], TN, preferred_element_type=f32)) or []
        return []

    items = [(t, h) for t in order for h in range(heads)]
    for step in steps_of(order[0]):
        step()
    ready = [scores(*it) for it in items[:3]]
    waiting, later = [], []
    for k, (t, h) in enumerate(items):
        if h == 0:
            place = order.index(t) + 1
            todo = steps_of(order[place]) if place < len(order) else []
        if h < heads - 3:
            count = -(-len(todo) // (heads - 3 - h))
            for step in todo[:count]:
                step()
            todo = todo[count:]
        for step in later[:4]:
            step()
        later = later[4:]
        if k + 3 < len(items):
            ready.append(scores(*items[k + 3]))
        st = ready.pop(0)
        e = jnp.exp2(st - jnp.max(st, axis=0, keepdims=True))
        waiting.append((t, h, jnp.concatenate([e, jnp.zeros((40, 256), f32)], axis=0).astype(bf16)))
        if len(waiting) > 3:
            later += mix(*waiting.pop(0))
    for args in waiting:
        later += mix(*args)
    for step in later:
        step()


def token_label(t, lab_ref, start):
    t = t - jnp.where(t >= 144, 144, jnp.where(t >= 72, 72, 0))
    n = lab_ref.shape[0]
    out = jnp.zeros(t.shape, jnp.int32)
    for r in range(6):
        lab = lab_ref[lax.rem(start + r + n, n)]
        out = jnp.where(t >= 12 * r, lab, out)
    return out


def fill_bias(bias_ref, lab_ref, start):
    kt = token_label(lax.broadcasted_iota(jnp.int32, (216, 256), 0), lab_ref, start)
    qt = token_label(lax.broadcasted_iota(jnp.int32, (216, 256), 1), lab_ref, start)
    bias_ref[...] = jnp.where(kt == qt, f32(0), f32(-1e30))


def vm():
    return pl.BlockSpec(memory_space=pltpu.VMEM)


def mega_kernel(
    lab_ref, x_hbm, g1, w1_hbm, o1_hbm, mg, mw_hbm, gc, wc_hbm, oc_hbm, sg, sw_hbm, g3, w3_hbm, o3_hbm,
    out_ref,
    w1, o1, mw, wc, oc, sw, w3, o3, wvt, wvtc,
    xa, xb, xw, nbuf, ebuf, sedge, jbuf, redge, sedge2, comb, hedge, sedge3,
    hx, xc, tmp, etmp, bias, q_s, k_s, vt_s, ot_s, qc, kc, vtc, otc, final,
    wsem, own_s, own8_s, s0a, r0a, s0b, r0b, own8_r,
    s1, r1, s1e, r1e, s2, r2, s2e, r2e, s3, r3, s3e, r3e, osem,
):
    i = lax.axis_index("lat")
    c = lax.axis_index("lon")
    n_lat = lax.axis_size("lat")
    n_lon = lax.axis_size("lon")
    o = lax.rem(i, 2)

    def dev(di, dc):
        return {"lat": lax.rem(i + di + n_lat, n_lat), "lon": lax.rem(c + dc + n_lon, n_lon)}

    def remote(src, dst, ssem, rsem, to):
        return pltpu.make_async_remote_copy(
            src_ref=src, dst_ref=dst, send_sem=ssem, recv_sem=rsem, device_id=to,
            device_id_type=pl.DeviceIdType.MESH,
        )

    own = pltpu.make_async_copy(
        x_hbm.at[:, :, pl.ds(pl.multiple_of(48 * (1 - o), 16), 48)], xa.at[:, 3:9], own_s
    )
    own.start()
    weights = [
        pltpu.make_async_copy(a, b, wsem.at[k])
        for k, (a, b) in enumerate(
            ((w1_hbm, w1), (o1_hbm, o1), (mw_hbm, mw), (wc_hbm, wc), (oc_hbm, oc), (sw_hbm, sw), (w3_hbm, w3), (o3_hbm, o3))
        )
    ]
    weights[0].start()
    weights[1].start()

    barrier = pltpu.get_barrier_semaphore()
    side = 1 - 2 * o
    for di, dc in ((-1, 0), (1, 0), (-2, 0), (2, 0), (0, -1), (0, 1), (-1, side), (1, side)):
        pl.semaphore_signal(barrier, inc=1, device_id=dev(di, dc), device_id_type=pl.DeviceIdType.MESH)
    pl.semaphore_wait(barrier, 8)

    def t0a(g):
        return remote(
            x_hbm.at[:, pl.ds(3 * g, 3), pl.ds(pl.multiple_of(48 * o, 16), 48)],
            xa.at[:, pl.ds(9 * (1 - g), 3)], s0a.at[1 - g], r0a.at[1 - g], dev(2 * g - 1, 0),
        )

    def t0b(g):
        return remote(
            x_hbm.at[:, pl.ds(3 * g, 3), pl.ds(pl.multiple_of(48 * (1 - o), 16), 8)],
            xb.at[:, pl.ds(9 * (1 - g), 3)], s0b.at[1 - g], r0b.at[1 - g], dev(2 * g - 1, -o),
        )

    def t0c_remote():
        return remote(x_hbm.at[:, :, 0:8], xb.at[:, 3:9], own8_s, own8_r, dev(0, -1))

    def t0c_local():
        return pltpu.make_async_copy(x_hbm.at[:, :, 48:56], xb.at[:, 3:9], own8_r)

    g_in = 1 - o
    for g in (0, 1):
        t0a(g).start()
        t0b(g).start()

    @pl.when(o == 0)
    def _():
        t0c_remote().start()

    @pl.when(o == 1)
    def _():
        t0c_local().start()

    for v in (vt_s, vtc):
        n, heads = v.shape[:2]
        v[:, :, 64:80, :] = jnp.ones((n, heads, 16, 256), bf16)
        v[:, :, :64, 128:256] = jnp.zeros((n, heads, 64, 128), bf16)
    fill_bias(bias.at[0], lab_ref, i * 6 - 3 + n_lat * 6)
    fill_bias(bias.at[1], lab_ref, i * 6 + 3)
    weights[0].wait()
    weights[1].wait()
    wvt[...] = w1[:, 1024:1536].T
    own.wait()

    @pl.when(o == 0)
    def _():
        t0c_remote().wait_recv()

    @pl.when(o == 1)
    def _():
        t0c_local().wait()

    fb = 3 * (1 - o)
    gb = 3 * o

    def chunk_to(k):
        far = jnp.where(o == 1, jnp.where(k == 0, -1, 1), jnp.where(k == 3, 1, -1))
        return lax.rem(k + 1 + 2 * o, 4), far

    def edge1(k):
        m, far = chunk_to(k)
        return remote(sedge.at[:, pl.ds(3 * k, 3)], ebuf.at[:, pl.ds(3 * m, 3)], s1e.at[k], r1e.at[m], dev(far, -o))

    def edge2(k):
        m, far = chunk_to(k)
        return remote(sedge2.at[:, pl.ds(3 * k, 3)], redge.at[:, pl.ds(3 * m, 3)], s2e.at[k], r2e.at[m], dev(far, 1 - o))

    rows1 = [
        remote(
            nbuf.at[k, :, pl.ds(12 * (1 - o), 3)], nbuf.at[k, :, pl.ds(12 * o, 3)], s1.at[k], r1.at[k], dev(2 - 4 * o, 0)
        )
        for k in range(2)
    ]
    rows2 = remote(
        jbuf.at[:, pl.ds(12 * o, 3)], jbuf.at[:, pl.ds(12 * (1 - o), 3)], s2, r2, dev(4 * o - 2, 0)
    )

    def group1(s, carry):
        g = (1 - o) * (1 - s) + o * s
        t0a(1 - g).wait_recv()
        t0b(1 - g).wait_recv()

        @pl.when(s == 0)
        def _():
            for copy in weights[2:]:
                copy.start()

        for lr in range(18):
            a = xa[lr // 6, 6 * g + lr % 6].astype(f32)
            b = xb[lr // 6, 6 * g + lr % 6].astype(f32)
            for w in range(3):
                xw[4 * g + w, 12 * lr : 12 * lr + 12, :] = a[6 + 12 * w : 18 + 12 * w]
            xw[4 * g + 3, 12 * lr : 12 * lr + 6, :] = a[42:48]
            xw[4 * g + 3, 12 * lr + 6 : 12 * lr + 12, :] = b[0:6]

        def finish(t, y):
            xw[4 * g + t] = xw[4 * g + t] + y
            if t == 0:
                for lr in range(18):
                    sedge[lr // 6, 6 * g + lr % 6] = xw[4 * g, 12 * lr : 12 * lr + 8, :].astype(bf16)
                edge1(2 * g).start()
                edge1(2 * g + 1).start()
            if t % 2 == 1:
                for lr in range(18):
                    pair = [xw[4 * g + w, 12 * lr : 12 * lr + 12, :] for w in (t - 1, t)]
                    nbuf[t // 2, lr // 6, fb + 6 * g + lr % 6] = jnp.concatenate(pair, axis=0).astype(bf16)

                @pl.when(s == 0)
                def _():
                    rows1[t // 2].start()

        hold = {}

        def begin(t):
            def take():
                hold[t] = xw[4 * g + t]

            return [take]

        attend_windows([0, 1, 2, 3], begin, finish, hold, g1[...], w1, wvt, o1, q_s, k_s, vt_s, ot_s, bias.at[g])
        return carry

    lax.fori_loop(0, 2, group1, 0)

    for copy in weights[2:6]:
        copy.wait()
    wvtc[...] = wc[:, 2048:3072].T
    for k in range(2):
        rows1[k].wait_recv()
    for k in range(4):
        edge1(k).wait_recv()
    for lr in range(18):
        l, rr = lr // 6, lr % 6
        for r in range(2):
            a = [nbuf[k, l, gb + 2 * rr + r].astype(f32) for k in range(2)]
            b = ebuf[l, 2 * rr + r].astype(f32)
            for j in range(4):
                for k in range(2):
                    tmp[lr % 2, r, j, 24 * k : 24 * k + 24] = a[k][:, 128 * j : 128 * j + 128]
                tmp[lr % 2, r, j, 48:56] = b[:, 128 * j : 128 * j + 128]
        for p in range(4):
            for j in range(4):
                v = tmp[lr % 2, p % 2, j, pl.ds(6 + p // 2, 24, stride=2), :]
                col = 512 * p + 128 * j
                for w in range(2):
                    hx[w, 12 * lr : 12 * lr + 12, col : col + 128] = v[12 * w : 12 * w + 12]

    hold = {}

    def merge(w):
        def stacked():
            hold[w] = norm(hx[w], mg[...])

        def product(c):
            m = jnp.dot(hold[w], mw[:, c : c + 256], preferred_element_type=f32)
            xc[w, :, c : c + 256] = m.astype(bf16).astype(f32)

        def take():
            hold[w] = xc[w]

        return [stacked] + [functools.partial(product, c) for c in range(0, 1024, 256)] + [take]

    def split(w, y):
        def stacked():
            hold[w] = norm((xc[w] + y).astype(bf16).astype(f32), sg[...])

        def product(c):
            hx[w, :, c : c + 256] = jnp.dot(hold[w], sw[:, c : c + 256], preferred_element_type=f32)

        def edges():
            for lr in range(18):
                l, rr = lr // 6, lr % 6
                for p in range(4):
                    for j in range(4):
                        col = 512 * p + 128 * j
                        etmp[lr, p % 2, j, pl.ds(p // 2, 3, stride=2), :] = hx[1, 12 * lr + 9 : 12 * lr + 12, col : col + 128]
                for r in range(2):
                    sp = jnp.concatenate([etmp[lr, r, j] for j in range(4)], axis=1)
                    sedge2[l, 2 * rr + r] = (ebuf[l, 2 * rr + r].astype(f32) + sp).astype(bf16)
            for k in range(4):
                edge2(k).start()

        steps = [stacked] + [functools.partial(product, c) for c in range(0, 2048, 256)]
        return steps + [edges] if w == 1 else steps

    attend_windows([1, 0], merge, split, hold, gc[...], wc, wvtc, oc, qc, kc, vtc, otc, None)
    for lr in range(18):
        l, rr = lr // 6, lr % 6
        for p in range(4):
            for j in range(4):
                col = 512 * p + 128 * j
                v = jnp.concatenate([hx[w, 12 * lr : 12 * lr + 12, col : col + 128] for w in range(2)], axis=0)
                tmp[lr % 2, p % 2, j, pl.ds(6 + p // 2, 24, stride=2), :] = v
        for r in range(2):
            sp = jnp.concatenate([tmp[lr % 2, r, j] for j in range(4)], axis=1)
            a = jnp.concatenate([nbuf[k, l, gb + 2 * rr + r].astype(f32) for k in range(2)], axis=0)
            jbuf[l, gb + 2 * rr + r] = (a + sp[0:48]).astype(bf16)
    rows2.start()

    weights[6].wait()
    weights[7].wait()
    wvt[...] = w3[:, 1024:1536].T

    def t3(g, half):
        return remote(
            comb.at[1 - o, half, :, pl.ds(9 * g, 3)], comb.at[1 - o, half, :, pl.ds(6 - 3 * g, 3)],
            s3.at[2 * g + half], r3.at[2 * (1 - g) + half], dev(2 * g - 1, 0),
        )

    def edge3(k):
        far = jnp.where(k == 0, -1, jnp.where(k == 3, 1, 0))
        m = lax.rem(k + 1, 2)
        return remote(sedge3.at[:, pl.ds(3 * k, 3)], hedge.at[:, pl.ds(3 * m, 3)], s3e.at[k], r3e.at[m], dev(far, 1))

    def group3(s, carry):
        g = o * (1 - s) + (1 - o) * s

        @pl.when(s == 1)
        def _():
            rows2.wait_recv()

        for lr in range(18):
            a = jbuf[lr // 6, fb + 6 * g + lr % 6].astype(f32)
            for w in range(1, 4):
                xw[4 * g + w, 12 * lr : 12 * lr + 12, :] = a[12 * w : 12 * w + 12]

        def finish(t, y):
            xw[4 * g + t] = xw[4 * g + t] + y
            if t == 3:
                for lr in range(18):
                    sedge3[lr // 6, 6 * g + lr % 6] = xw[4 * g + 3, 12 * lr + 4 : 12 * lr + 12, :].astype(bf16)

                @pl.when(o == 0)
                def _():
                    edge3(2 * g).start()
                    edge3(2 * g + 1).start()

            if t % 2 == 0:
                for lr in range(18):
                    pair = [xw[4 * g + w, 12 * lr : 12 * lr + 12, :] for w in (t, t + 1)]
                    comb[1 - o, t // 2, lr // 6, 6 * g + lr % 6] = jnp.concatenate(pair, axis=0).astype(bf16)
                t3(g, t // 2).start()

        hold = {}

        def begin(t):
            def landed():
                for m in range(2):
                    remote(
                        sedge2.at[:, pl.ds(0, 3)], redge.at[:, pl.ds(6 * g + 3 * m, 3)], s2e.at[0], r2e.at[2 * g + m], dev(1, 0)
                    ).wait_recv()
                for lr in range(18):
                    xw[4 * g, 12 * lr : 12 * lr + 6, :] = redge[lr // 6, 6 * g + lr % 6].astype(f32)[0:6]
                    xw[4 * g, 12 * lr + 6 : 12 * lr + 12, :] = jbuf[lr // 6, fb + 6 * g + lr % 6].astype(f32)[6:12]

            def take():
                hold[t] = xw[4 * g + t]

            return [landed, take] if t == 0 else [take]

        attend_windows([3, 2, 1, 0], begin, finish, hold, g3[...], w3, wvt, o3, q_s, k_s, vt_s, ot_s, bias.at[g])
        return carry

    lax.fori_loop(0, 2, group3, 0)

    def out_copy(b):
        return pltpu.make_async_copy(final.at[:, pl.ds(3 * b, 3)], out_ref.at[:, pl.ds(3 * b, 3)], osem.at[b])

    def assemble(s, carry):
        b = o * (1 - s) + (1 - o) * s
        for half in range(2):
            remote(
                comb.at[o, half, :, pl.ds(0, 3)], comb.at[o, half, :, pl.ds(3 + 3 * b, 3)], s3.at[0], r3.at[2 * b + half],
                dev(1, 0),
            ).wait_recv()
        remote(sedge3.at[:, pl.ds(0, 3)], hedge.at[:, pl.ds(3 * b, 3)], s3e.at[0], r3e.at[b], dev(0, 1)).wait_recv()
        for lr in range(9):
            l, r = lr // 3, 3 * b + lr % 3
            halves = [comb[k, half, l, r + 3].astype(f32) for k in range(2) for half in range(2)]
            parts = [hedge[l, r].astype(f32)[2:8]] + halves[:3] + [halves[3][0:18]]
            final[l, r] = jnp.concatenate(parts, axis=0).astype(bf16)
        out_copy(b).start()
        return carry

    lax.fori_loop(0, 2, assemble, 0)

    for g in (0, 1):
        t0a(1 - g).wait_send()
        t0b(1 - g).wait_send()
        t3(g, 0).wait_send()
        t3(g, 1).wait_send()
        out_copy(g).wait()
    for k in range(4):
        edge1(k).wait_send()
        edge2(k).wait_send()
    for k in range(2):
        rows1[k].wait_send()
    rows2.wait_send()

    @pl.when(o == 0)
    def _():
        t0c_remote().wait_send()
        for k in range(4):
            edge3(k).wait_send()


def mega_call(x, lab, g1, w1, o1, mg, mw, gc, wc, oc, sg, sw, g3, w3, o3):
    V = vm()
    H = pl.BlockSpec(memory_space=pl.ANY)
    B = lambda *s: pltpu.VMEM(s, bf16)
    F = lambda *s: pltpu.VMEM(s, f32)
    D = pltpu.SemaphoreType.DMA
    weights = [B(*a.shape) for a in (w1, o1, mw, wc, oc, sw, w3, o3)]
    scratch = weights + [
        B(512, 512), B(1024, 1024),
        B(3, 12, 48, 512), B(3, 12, 8, 512), F(8, 216, 512), B(2, 3, 15, 24, 512), B(3, 12, 8, 512), B(3, 12, 8, 512),
        B(3, 15, 48, 512), B(3, 12, 8, 512), B(3, 12, 8, 512), B(2, 2, 3, 12, 24, 512), B(3, 6, 8, 512), B(3, 12, 8, 512),
        F(2, 216, 2048), F(2, 216, 1024), F(2, 2, 4, 56, 128), F(18, 2, 4, 8, 128), F(2, 216, 256),
        B(4, 256, 512), B(4, 224, 512), B(4, 8, 80, 256), B(4, 512, 216),
        B(2, 256, 1024), B(2, 224, 1024), B(2, 16, 80, 256), B(2, 1024, 216), B(3, 6, 96, 512),
        D((8,)), D, D, D((2,)), D((2,)), D((2,)), D((2,)), D,
        D((2,)), D((2,)), D((4,)), D((4,)), D, D, D((4,)), D((4,)), D((4,)), D((4,)), D((4,)), D((2,)), D((2,)),
    ]
    row = lambda g: g.reshape(1, -1)
    return pl.pallas_call(
        mega_kernel,
        out_shape=jax.ShapeDtypeStruct(x.shape, bf16),
        in_specs=[pl.BlockSpec(memory_space=pltpu.SMEM), H, V, H, H, V, H, V, H, H, V, H, V, H, H],
        out_specs=H,
        scratch_shapes=scratch,
        compiler_params=pltpu.CompilerParams(
            vmem_limit_bytes=67043328, collective_id=0, has_side_effects=True
        ),
        name="section",
    )(lab, x, row(g1), w1, o1, row(mg), mw, row(gc), wc, oc, row(sg), sw, row(g3), w3, o3)


def solution(mesh):
    return jax.shard_map(
        mega_call,
        mesh=mesh,
        in_specs=(P("rep", "lat", "lon", None),) + (P(),) * 14,
        out_specs=P("rep", "lat", "lon", None),
        check_vma=False,
    )
```

```python
import functools
import jax
import jax.numpy as jnp
from jax import lax
from jax.experimental import pallas as pl
from jax.experimental.pallas import tpu as pltpu
from jax.sharding import PartitionSpec as P

NT = (((1,), (1,)), ((), ()))
TN = (((0,), (0,)), ((), ()))
f32 = jnp.float32
bf16 = jnp.bfloat16


def norm(x, g):
    c = jnp.mean(x, axis=-1, keepdims=True)
    d = x - c
    s = jnp.mean(d * d, axis=-1, keepdims=True)
    return (d * lax.rsqrt(s + 1e-05) * g).astype(bf16)


LOG2E = 1.4426950408889634


def attend_windows(order, begin, finish, hold, g, wqkv_ref, wvt_ref, wo_ref, q_s, k_s, vt_s, ot_s, bias_ref):
    E = wqkv_ref.shape[0]
    heads = E // 64
    lane = lax.broadcasted_iota(jnp.int32, (256, 128), 1)

    def steps_of(t):
        def normed():
            hold[t] = norm(hold[t], g)

        def query(c):
            y = jnp.dot(hold[t], wqkv_ref[:, c : c + 256], preferred_element_type=f32)
            q_s[t, :216, c : c + 256] = (y * (0.125 * LOG2E)).astype(bf16)

        def key(c):
            y = jnp.dot(hold[t], wqkv_ref[:, E + c : E + c + 256], preferred_element_type=f32)
            k_s[t, :216, c : c + 256] = y.astype(bf16)

        def value(c):
            y = lax.dot_general(wvt_ref[c : c + 256, :], hold[t], NT, preferred_element_type=f32).astype(bf16)
            for h in range(4):
                vt_s[t, c // 64 + h, :64, :216] = y[64 * h : 64 * h + 64]

        steps = list(begin(t)) + [normed]
        for c in range(0, E, 256):
            steps += [functools.partial(f, c) for f in (query, key, value)]
        return steps

    def scores(t, h):
        hp = 128 * (h // 2)
        qm = jnp.where((lane >= 64) if h % 2 else (lane < 64), q_s[t, :, hp : hp + 128], bf16(0))
        st = lax.dot_general(k_s[t, :, hp : hp + 128], qm, NT, preferred_element_type=f32)[:216]
        return st if bias_ref is None else st + bias_ref[...]

    def mix(t, h, e):
        ot = jnp.dot(vt_s[t, h], e, preferred_element_type=f32)
        ot_s[t, 64 * h : 64 * h + 64, :] = (ot[:64] * (1.0 / ot[64:65])).astype(bf16)[:, :216]
        if h == heads - 1:
            return finish(t, lax.dot_general(ot_s[t], wo_ref[...], TN, preferred_element_type=f32)) or []
        return []

    items = [(t, h) for t in order for h in range(heads)]
    for step in steps_of(order[0]):
        step()
    ready = [scores(*it) for it in items[:3]]
    waiting, later = [], []
    for k, (t, h) in enumerate(items):
        if h == 0:
            place = order.index(t) + 1
            todo = steps_of(order[place]) if place < len(order) else []
        if h < heads - 3:
            count = -(-len(todo) // (heads - 3 - h))
            for step in todo[:count]:
                step()
            todo = todo[count:]
        for step in later[:4]:
            step()
        later = later[4:]
        if k + 3 < len(items):
            ready.append(scores(*items[k + 3]))
        st = ready.pop(0)
        e = jnp.exp2(st - jnp.max(st, axis=0, keepdims=True))
        waiting.append((t, h, jnp.concatenate([e, jnp.zeros((40, 256), f32)], axis=0).astype(bf16)))
        if len(waiting) > 3:
            later += mix(*waiting.pop(0))
    for args in waiting:
        later += mix(*args)
    for step in later:
        step()


def token_label(t, lab_ref, start):
    t = t - jnp.where(t >= 144, 144, jnp.where(t >= 72, 72, 0))
    n = lab_ref.shape[0]
    out = jnp.zeros(t.shape, jnp.int32)
    for r in range(6):
        lab = lab_ref[lax.rem(start + r + n, n)]
        out = jnp.where(t >= 12 * r, lab, out)
    return out


def fill_bias(bias_ref, lab_ref, start):
    kt = token_label(lax.broadcasted_iota(jnp.int32, (216, 256), 0), lab_ref, start)
    qt = token_label(lax.broadcasted_iota(jnp.int32, (216, 256), 1), lab_ref, start)
    bias_ref[...] = jnp.where(kt == qt, f32(0), f32(-1e30))


def vm():
    return pl.BlockSpec(memory_space=pltpu.VMEM)


def mega_kernel(
    lab_ref, x_hbm, g1, w1_hbm, o1_hbm, mg, mw_hbm, gc, wc_hbm, oc_hbm, sg, sw_hbm, g3, w3_hbm, o3_hbm,
    out_ref,
    w1, o1, mw, wc, oc, sw, w3, o3, wvt, wvtc,
    xa, xb, xw, nbuf, ebuf, sedge, jbuf, redge, sedge2, comb, hedge, sedge3,
    hx, xc, tmp, etmp, bias, q_s, k_s, vt_s, ot_s, qc, kc, vtc, otc, final,
    wsem, own_s, own8_s, s0a, r0a, s0b, r0b, own8_r,
    s1, r1, s1e, r1e, s2, r2, s2e, r2e, s3, r3, s3e, r3e, osem,
):
    i = lax.axis_index("lat")
    c = lax.axis_index("lon")
    n_lat = lax.axis_size("lat")
    n_lon = lax.axis_size("lon")
    o = lax.rem(i, 2)

    def dev(di, dc):
        return {"lat": lax.rem(i + di + n_lat, n_lat), "lon": lax.rem(c + dc + n_lon, n_lon)}

    def remote(src, dst, ssem, rsem, to):
        return pltpu.make_async_remote_copy(
            src_ref=src, dst_ref=dst, send_sem=ssem, recv_sem=rsem, device_id=to,
            device_id_type=pl.DeviceIdType.MESH,
        )

    own = pltpu.make_async_copy(
        x_hbm.at[:, :, pl.ds(pl.multiple_of(48 * (1 - o), 16), 48)], xa.at[:, 3:9], own_s
    )
    own.start()
    weights = [
        pltpu.make_async_copy(a, b, wsem.at[k])
        for k, (a, b) in enumerate(
            ((w1_hbm, w1), (o1_hbm, o1), (mw_hbm, mw), (wc_hbm, wc), (oc_hbm, oc), (sw_hbm, sw), (w3_hbm, w3), (o3_hbm, o3))
        )
    ]
    weights[0].start()
    weights[1].start()

    barrier = pltpu.get_barrier_semaphore()
    side = 1 - 2 * o
    for di, dc in ((-1, 0), (1, 0), (-2, 0), (2, 0), (0, -1), (0, 1), (-1, side), (1, side)):
        pl.semaphore_signal(barrier, inc=1, device_id=dev(di, dc), device_id_type=pl.DeviceIdType.MESH)
    pl.semaphore_wait(barrier, 8)

    def t0a(g):
        return remote(
            x_hbm.at[:, pl.ds(3 * g, 3), pl.ds(pl.multiple_of(48 * o, 16), 48)],
            xa.at[:, pl.ds(9 * (1 - g), 3)], s0a.at[1 - g], r0a.at[1 - g], dev(2 * g - 1, 0),
        )

    def t0b(g):
        return remote(
            x_hbm.at[:, pl.ds(3 * g, 3), pl.ds(pl.multiple_of(48 * (1 - o), 16), 8)],
            xb.at[:, pl.ds(9 * (1 - g), 3)], s0b.at[1 - g], r0b.at[1 - g], dev(2 * g - 1, -o),
        )

    def t0c_remote():
        return remote(x_hbm.at[:, :, 0:8], xb.at[:, 3:9], own8_s, own8_r, dev(0, -1))

    def t0c_local():
        return pltpu.make_async_copy(x_hbm.at[:, :, 48:56], xb.at[:, 3:9], own8_r)

    g_in = 1 - o
    for g in (0, 1):
        t0a(g).start()
        t0b(g).start()

    @pl.when(o == 0)
    def _():
        t0c_remote().start()

    @pl.when(o == 1)
    def _():
        t0c_local().start()

    for v in (vt_s, vtc):
        n, heads = v.shape[:2]
        v[:, :, 64:80, :] = jnp.ones((n, heads, 16, 256), bf16)
        v[:, :, :64, 128:256] = jnp.zeros((n, heads, 64, 128), bf16)
    fill_bias(bias.at[0], lab_ref, i * 6 - 3 + n_lat * 6)
    fill_bias(bias.at[1], lab_ref, i * 6 + 3)
    weights[0].wait()
    weights[1].wait()
    wvt[...] = w1[:, 1024:1536].T
    own.wait()

    @pl.when(o == 0)
    def _():
        t0c_remote().wait_recv()

    @pl.when(o == 1)
    def _():
        t0c_local().wait()

    fb = 3 * (1 - o)
    gb = 3 * o

    def chunk_to(k):
        far = jnp.where(o == 1, jnp.where(k == 0, -1, 1), jnp.where(k == 3, 1, -1))
        return lax.rem(k + 1 + 2 * o, 4), far

    def edge1(k):
        m, far = chunk_to(k)
        return remote(sedge.at[:, pl.ds(3 * k, 3)], ebuf.at[:, pl.ds(3 * m, 3)], s1e.at[k], r1e.at[m], dev(far, -o))

    def edge2(k):
        m, far = chunk_to(k)
        return remote(sedge2.at[:, pl.ds(3 * k, 3)], redge.at[:, pl.ds(3 * m, 3)], s2e.at[k], r2e.at[m], dev(far, 1 - o))

    rows1 = [
        remote(
            nbuf.at[k, :, pl.ds(12 * (1 - o), 3)], nbuf.at[k, :, pl.ds(12 * o, 3)], s1.at[k], r1.at[k], dev(2 - 4 * o, 0)
        )
        for k in range(2)
    ]
    rows2 = [
        remote(
            jbuf.at[k, :, pl.ds(12 * o, 3)], jbuf.at[k, :, pl.ds(12 * (1 - o), 3)], s2.at[k], r2.at[k], dev(4 * o - 2, 0)
        )
        for k in range(2)
    ]

    def group1(s, carry):
        g = (1 - o) * (1 - s) + o * s
        t0a(1 - g).wait_recv()
        t0b(1 - g).wait_recv()

        @pl.when(s == 0)
        def _():
            for copy in weights[2:]:
                copy.start()

        for lr in range(18):
            a = xa[lr // 6, 6 * g + lr % 6].astype(f32)
            b = xb[lr // 6, 6 * g + lr % 6].astype(f32)
            for w in range(3):
                xw[4 * g + w, 12 * lr : 12 * lr + 12, :] = a[6 + 12 * w : 18 + 12 * w]
            xw[4 * g + 3, 12 * lr : 12 * lr + 6, :] = a[42:48]
            xw[4 * g + 3, 12 * lr + 6 : 12 * lr + 12, :] = b[0:6]

        def finish(t, y):
            xw[4 * g + t] = xw[4 * g + t] + y
            if t == 0:
                for lr in range(18):
                    sedge[lr // 6, 6 * g + lr % 6] = xw[4 * g, 12 * lr : 12 * lr + 8, :].astype(bf16)
                edge1(2 * g).start()
                edge1(2 * g + 1).start()
            if t % 2 == 1:
                for lr in range(18):
                    pair = [xw[4 * g + w, 12 * lr : 12 * lr + 12, :] for w in (t - 1, t)]
                    nbuf[t // 2, lr // 6, fb + 6 * g + lr % 6] = jnp.concatenate(pair, axis=0).astype(bf16)

                @pl.when(s == 0)
                def _():
                    rows1[t // 2].start()

        hold = {}

        def begin(t):
            def take():
                hold[t] = xw[4 * g + t]

            return [take]

        attend_windows([0, 1, 2, 3], begin, finish, hold, g1[...], w1, wvt, o1, q_s, k_s, vt_s, ot_s, bias.at[g])
        return carry

    lax.fori_loop(0, 2, group1, 0)

    for copy in weights[2:6]:
        copy.wait()
    wvtc[...] = wc[:, 2048:3072].T
    for k in range(2):
        rows1[k].wait_recv()
    for k in range(4):
        edge1(k).wait_recv()
    for lr in range(18):
        l, rr = lr // 6, lr % 6
        for r in range(2):
            a = [nbuf[k, l, gb + 2 * rr + r].astype(f32) for k in range(2)]
            b = ebuf[l, 2 * rr + r].astype(f32)
            for j in range(4):
                for k in range(2):
                    tmp[lr % 2, r, j, 24 * k : 24 * k + 24] = a[k][:, 128 * j : 128 * j + 128]
                tmp[lr % 2, r, j, 48:56] = b[:, 128 * j : 128 * j + 128]
        for p in range(4):
            for j in range(4):
                v = tmp[lr % 2, p % 2, j, pl.ds(6 + p // 2, 24, stride=2), :]
                col = 512 * p + 128 * j
                for w in range(2):
                    hx[w, 12 * lr : 12 * lr + 12, col : col + 128] = v[12 * w : 12 * w + 12]

    hold = {}

    def merge(w):
        def stacked():
            hold[w] = norm(hx[w], mg[...])

        def product(c):
            m = jnp.dot(hold[w], mw[:, c : c + 256], preferred_element_type=f32)
            xc[w, :, c : c + 256] = m.astype(bf16).astype(f32)

        def take():
            hold[w] = xc[w]

        return [stacked] + [functools.partial(product, c) for c in range(0, 1024, 256)] + [take]

    def split(w, y):
        def stacked():
            hold[w] = norm((xc[w] + y).astype(bf16).astype(f32), sg[...])

        def product(c):
            hx[w, :, c : c + 256] = jnp.dot(hold[w], sw[:, c : c + 256], preferred_element_type=f32)

        def edges():
            for lr in range(18):
                l, rr = lr // 6, lr % 6
                for p in range(4):
                    for j in range(4):
                        col = 512 * p + 128 * j
                        etmp[lr, p % 2, j, pl.ds(p // 2, 3, stride=2), :] = hx[1, 12 * lr + 9 : 12 * lr + 12, col : col + 128]
                for r in range(2):
                    sp = jnp.concatenate([etmp[lr, r, j] for j in range(4)], axis=1)
                    sedge2[l, 2 * rr + r] = (ebuf[l, 2 * rr + r].astype(f32) + sp).astype(bf16)
            for k in range(4):
                edge2(k).start()

        steps = [stacked] + [functools.partial(product, c) for c in range(0, 2048, 256)]
        return steps + [edges] if w == 1 else steps

    attend_windows([1, 0], merge, split, hold, gc[...], wc, wvtc, oc, qc, kc, vtc, otc, None)
    for lr in range(18):
        l, rr = lr // 6, lr % 6
        for p in range(4):
            for j in range(4):
                col = 512 * p + 128 * j
                v = jnp.concatenate([hx[w, 12 * lr : 12 * lr + 12, col : col + 128] for w in range(2)], axis=0)
                tmp[lr % 2, p % 2, j, pl.ds(6 + p // 2, 24, stride=2), :] = v
        for r in range(2):
            sp = jnp.concatenate([tmp[lr % 2, r, j] for j in range(4)], axis=1)
            for k in range(2):
                a = nbuf[k, l, gb + 2 * rr + r].astype(f32)
                jbuf[k, l, gb + 2 * rr + r] = (a + sp[24 * k : 24 * k + 24]).astype(bf16)
    rows2[1].start()
    rows2[0].start()

    weights[6].wait()
    weights[7].wait()
    wvt[...] = w3[:, 1024:1536].T

    def t3(g, half):
        return remote(
            comb.at[1 - o, half, :, pl.ds(9 * g, 3)], comb.at[1 - o, half, :, pl.ds(6 - 3 * g, 3)],
            s3.at[2 * g + half], r3.at[2 * (1 - g) + half], dev(2 * g - 1, 0),
        )

    def edge3(k):
        far = jnp.where(k == 0, -1, jnp.where(k == 3, 1, 0))
        m = lax.rem(k + 1, 2)
        return remote(sedge3.at[:, pl.ds(3 * k, 3)], hedge.at[:, pl.ds(3 * m, 3)], s3e.at[k], r3e.at[m], dev(far, 1))

    def group3(s, carry):
        g = o * (1 - s) + (1 - o) * s

        @pl.when(s == 1)
        def _():
            rows2[1].wait_recv()

        for lr in range(18):
            a = jbuf[1, lr // 6, fb + 6 * g + lr % 6].astype(f32)
            for w in range(2):
                xw[4 * g + 2 + w, 12 * lr : 12 * lr + 12, :] = a[12 * w : 12 * w + 12]

        def finish(t, y):
            xw[4 * g + t] = xw[4 * g + t] + y
            if t == 3:
                for lr in range(18):
                    sedge3[lr // 6, 6 * g + lr % 6] = xw[4 * g + 3, 12 * lr + 4 : 12 * lr + 12, :].astype(bf16)

                @pl.when(o == 0)
                def _():
                    edge3(2 * g).start()
                    edge3(2 * g + 1).start()

            if t % 2 == 0:
                for lr in range(18):
                    pair = [xw[4 * g + w, 12 * lr : 12 * lr + 12, :] for w in (t, t + 1)]
                    comb[1 - o, t // 2, lr // 6, 6 * g + lr % 6] = jnp.concatenate(pair, axis=0).astype(bf16)
                t3(g, t // 2).start()

        hold = {}

        def begin(t):
            def half():
                @pl.when(s == 1)
                def _():
                    rows2[0].wait_recv()

                for lr in range(18):
                    a = jbuf[0, lr // 6, fb + 6 * g + lr % 6].astype(f32)
                    xw[4 * g + 1, 12 * lr : 12 * lr + 12, :] = a[12:24]

            def landed():
                for m in range(2):
                    remote(
                        sedge2.at[:, pl.ds(0, 3)], redge.at[:, pl.ds(6 * g + 3 * m, 3)], s2e.at[0], r2e.at[2 * g + m], dev(1, 0)
                    ).wait_recv()
                for lr in range(18):
                    xw[4 * g, 12 * lr : 12 * lr + 6, :] = redge[lr // 6, 6 * g + lr % 6].astype(f32)[0:6]
                    xw[4 * g, 12 * lr + 6 : 12 * lr + 12, :] = jbuf[0, lr // 6, fb + 6 * g + lr % 6].astype(f32)[6:12]

            def take():
                hold[t] = xw[4 * g + t]

            return {0: [landed], 1: [half]}.get(t, []) + [take]

        attend_windows([3, 2, 1, 0], begin, finish, hold, g3[...], w3, wvt, o3, q_s, k_s, vt_s, ot_s, bias.at[g])
        return carry

    lax.fori_loop(0, 2, group3, 0)

    def out_copy(b):
        return pltpu.make_async_copy(final.at[:, pl.ds(3 * b, 3)], out_ref.at[:, pl.ds(3 * b, 3)], osem.at[b])

    def assemble(s, carry):
        b = o * (1 - s) + (1 - o) * s
        for half in range(2):
            remote(
                comb.at[o, half, :, pl.ds(0, 3)], comb.at[o, half, :, pl.ds(3 + 3 * b, 3)], s3.at[0], r3.at[2 * b + half],
                dev(1, 0),
            ).wait_recv()
        remote(sedge3.at[:, pl.ds(0, 3)], hedge.at[:, pl.ds(3 * b, 3)], s3e.at[0], r3e.at[b], dev(0, 1)).wait_recv()
        for lr in range(9):
            l, r = lr // 3, 3 * b + lr % 3
            halves = [comb[k, half, l, r + 3].astype(f32) for k in range(2) for half in range(2)]
            parts = [hedge[l, r].astype(f32)[2:8]] + halves[:3] + [halves[3][0:18]]
            final[l, r] = jnp.concatenate(parts, axis=0).astype(bf16)
        out_copy(b).start()
        return carry

    lax.fori_loop(0, 2, assemble, 0)

    for g in (0, 1):
        t0a(1 - g).wait_send()
        t0b(1 - g).wait_send()
        t3(g, 0).wait_send()
        t3(g, 1).wait_send()
        out_copy(g).wait()
    for k in range(4):
        edge1(k).wait_send()
        edge2(k).wait_send()
    for k in range(2):
        rows1[k].wait_send()
    for k in range(2):
        rows2[k].wait_send()

    @pl.when(o == 0)
    def _():
        t0c_remote().wait_send()
        for k in range(4):
            edge3(k).wait_send()


def mega_call(x, lab, g1, w1, o1, mg, mw, gc, wc, oc, sg, sw, g3, w3, o3):
    V = vm()
    H = pl.BlockSpec(memory_space=pl.ANY)
    B = lambda *s: pltpu.VMEM(s, bf16)
    F = lambda *s: pltpu.VMEM(s, f32)
    D = pltpu.SemaphoreType.DMA
    weights = [B(*a.shape) for a in (w1, o1, mw, wc, oc, sw, w3, o3)]
    scratch = weights + [
        B(512, 512), B(1024, 1024),
        B(3, 12, 48, 512), B(3, 12, 8, 512), F(8, 216, 512), B(2, 3, 15, 24, 512), B(3, 12, 8, 512), B(3, 12, 8, 512),
        B(2, 3, 15, 24, 512), B(3, 12, 8, 512), B(3, 12, 8, 512), B(2, 2, 3, 12, 24, 512), B(3, 6, 8, 512), B(3, 12, 8, 512),
        F(2, 216, 2048), F(2, 216, 1024), F(2, 2, 4, 56, 128), F(18, 2, 4, 8, 128), F(2, 216, 256),
        B(4, 256, 512), B(4, 224, 512), B(4, 8, 80, 256), B(4, 512, 216),
        B(2, 256, 1024), B(2, 224, 1024), B(2, 16, 80, 256), B(2, 1024, 216), B(3, 6, 96, 512),
        D((8,)), D, D, D((2,)), D((2,)), D((2,)), D((2,)), D,
        D((2,)), D((2,)), D((4,)), D((4,)), D((2,)), D((2,)), D((4,)), D((4,)), D((4,)), D((4,)), D((4,)), D((2,)), D((2,)),
    ]
    row = lambda g: g.reshape(1, -1)
    return pl.pallas_call(
        mega_kernel,
        out_shape=jax.ShapeDtypeStruct(x.shape, bf16),
        in_specs=[pl.BlockSpec(memory_space=pltpu.SMEM), H, V, H, H, V, H, V, H, H, V, H, V, H, H],
        out_specs=H,
        scratch_shapes=scratch,
        compiler_params=pltpu.CompilerParams(
            vmem_limit_bytes=67043328, collective_id=0, has_side_effects=True
        ),
        name="section",
    )(lab, x, row(g1), w1, o1, row(mg), mw, row(gc), wc, oc, row(sg), sw, row(g3), w3, o3)


def solution(mesh):
    return jax.shard_map(
        mega_call,
        mesh=mesh,
        in_specs=(P("rep", "lat", "lon", None),) + (P(),) * 14,
        out_specs=P("rep", "lat", "lon", None),
        check_vma=False,
    )
```
